256 devices in a mesh: tm: 256 (over z, x, y, core).
Axes of the slice: x: 4, y: 4, z: 8, core: 2. Of those that a mesh axis runs over, the one named last changes fastest.
Arguments:
- transition: float32 [256, 256], replicated, may hold values from -1 to 1
- noise_var: float32 [256], replicated, may hold values from 0.001 to 0.1
- prior_mean: float32 [256], replicated, may hold values from -6 to 6
- prior_var: float32 [256], replicated, may hold values from 0.5 to 2
- obs_op: bfloat16 [256, 8, 128, 128], P('tm'), may hold values from -0.5 to 0.5
- obs_value: float32 [256, 8, 128], P('tm'), may hold values from -18 to 18
- obs_noise: float32 [256, 8, 128], P('tm'), may hold values from 10 to 100
- obs_block: int32 [256, 8], P('tm'), may hold values from 0 to 1
- obs_count: int32 [256], P('tm'), may hold values from 1 to 8, as said below
Outputs:
- smoothed_mean: float32 [256, 256], P('tm')
- smoothed_var: float32 [256, 256], P('tm')
The draws below stay inside these ranges and needn't reach their ends.
Inputs may be any that keep to these rules, and one draw needn't show every extreme that they name: Only the first obs_count[t] slots of step t carry observations; some step reports all 8.
All inputs are finite; a program needn't handle non-finite values.
Results may differ from the reference program's by a relative error of at most 0.024.
Values sent between devices are 32-bit elements; how exact they have to be, the bound alone decides.
No kernel may reach another device: no remote copies, remote signals or barrier semaphores. Data moves between devices by JAX's collectives and lax.ppermute only.
A program may use at most 192 MiB of HBM per device.

```python
import math
import jax
import jax.numpy as jnp
from jax import lax

S = 256
BLOCK = 128
NB = 2
MAXB = 8
TIME = 256


def draw_transition(key, part):
    rate_key = jax.random.fold_in(key, 11)
    mix_key = jax.random.fold_in(key, 12)
    rates = jnp.exp(jax.random.uniform(rate_key, (S,), jnp.float32, math.log(0.5 / TIME), math.log(1.0 / 30.0)))
    mixing = jax.random.normal(mix_key, (S, S), jnp.float32) * (0.15 / math.sqrt(S))
    return jnp.diag(jnp.exp(-rates)) + (mixing - mixing.T)


def draw_obs_count(key, part):
    level = jax.random.randint(jax.random.fold_in(key, 21), (TIME,), 0, MAXB)
    position = jnp.arange(TIME, dtype=jnp.int32)
    rising = 1 + level * (position + 1) // TIME
    return jnp.where(position == TIME - 1, MAXB, rising).astype(jnp.int32)


def set_ends(result, stream_key, smallest, high):
    place = [jax.random.randint(jax.random.fold_in(stream_key, axis), (), 0, length) for axis, length in enumerate(result.shape)]
    widest = result.shape.index(max(result.shape))
    next_to = place[:widest] + [(place[widest] + 1) % result.shape[widest]] + place[widest + 1:]
    return result.at[tuple(place)].set(smallest).at[tuple(next_to)].set(high)


def level_of(stream_key, dims, pieces, least, largest):
    loudness = 1.0
    for axis_at, parts in pieces:
        steps = jax.random.uniform(jax.random.fold_in(jax.random.fold_in(stream_key, 6), axis_at), (parts,), jnp.float32, least / len(pieces), largest / len(pieces))
        loudness = loudness * jnp.repeat(jnp.exp(steps), dims[axis_at] // parts).reshape((-1,) + (1,) * (len(dims) - 1 - axis_at))
    return loudness


def normal_values(own_key, shape, scale, most, cuts=(), kind=jnp.bfloat16):
    loudness = level_of(own_key, shape, cuts, -0.22, 0.18) if cuts else 1.0
    result = jax.random.normal(own_key, shape, jnp.float32) * scale * loudness
    return jnp.minimum(jnp.maximum(result, -most), most).astype(kind)


def setup_inputs(seed: int = 0) -> dict:
    key_of = jax.random.split(jax.random.key(seed), 10)
    transition = draw_transition(jax.random.fold_in(key_of[9], 71), 0)
    noise_var = jnp.clip(jnp.exp(jax.random.uniform(key_of[1], (S,), jnp.float32, math.log(0.001), math.log(0.1))), 0.001, 0.1)
    prior_mean = normal_values(key_of[2], (S,), 1.0, 6.0, (), jnp.float32)
    prior_var = jnp.clip(jnp.exp(jax.random.uniform(key_of[3], (S,), jnp.float32, math.log(0.5), math.log(2.0))), 0.5, 2.0)
    obs_op = normal_values(key_of[4], (TIME, MAXB, BLOCK, BLOCK), BLOCK ** -0.5, 0.5, ((0, 256),))
    obs_value = normal_values(key_of[5], (TIME, MAXB, BLOCK), 3.0, 18.0, ((0, 256),), jnp.float32)
    obs_noise = jnp.clip(jnp.exp(math.log(100.0) - 2.3025851 * jax.random.uniform(key_of[6], (TIME, MAXB, BLOCK), jnp.float32) ** level_of(key_of[6], (TIME, MAXB, BLOCK), ((0, 256),), -0.2, 0.2)), 10.0, 100.0)
    obs_block = set_ends(jax.random.randint(key_of[7], (TIME, MAXB), 0, NB), jax.random.fold_in(key_of[7], 1), 0, NB - 1).astype(jnp.int32)
    obs_count = draw_obs_count(jax.random.fold_in(key_of[9], 71), 0)
    return {"transition": transition, "noise_var": noise_var, "prior_mean": prior_mean, "prior_var": prior_var, "obs_op": obs_op, "obs_value": obs_value, "obs_noise": obs_noise, "obs_block": obs_block, "obs_count": obs_count}


precise = lax.Precision.HIGHEST

def product(left, right):
    return jnp.dot(left.astype(jnp.float32), right.astype(jnp.float32), precision=precise, preferred_element_type=jnp.float32)

def step_information(obs_op, obs_value, obs_noise, obs_block, obs_count, nblocks):
    slots = obs_op.shape[0]
    width = obs_op.shape[2]
    active = (jnp.arange(slots, dtype=jnp.int32) < obs_count).astype(jnp.float32)
    chosen = (obs_block[:, None] == jnp.arange(nblocks, dtype=jnp.int32)[None, :]).astype(jnp.float32) * active[:, None]
    wide_op = obs_op.astype(jnp.float32)
    scaled = (wide_op / obs_noise[:, :, None]).astype(jnp.bfloat16)
    scaled = lax.optimization_barrier(scaled).astype(jnp.float32)
    slot_info = jnp.einsum('msi,msj->mij', scaled, wide_op, precision=precise)
    slot_shift = jnp.einsum('msi,ms->mi', wide_op, obs_value / obs_noise, precision=precise)
    block_info = jnp.einsum('ma,mij->aij', chosen, slot_info, precision=precise)
    block_shift = jnp.einsum('ma,mi->ai', chosen, slot_shift, precision=precise)
    dense = jnp.einsum('aij,ac->aicj', block_info, jnp.eye(nblocks, dtype=jnp.float32), precision=precise)
    return (dense.reshape(nblocks * width, nblocks * width), block_shift.reshape(nblocks * width))

def reference(transition, noise_var, prior_mean, prior_var, obs_op, obs_value, obs_noise, obs_block, obs_count):
    width = transition.shape[0]
    nblocks = width // BLOCK
    eye = jnp.eye(width, dtype=jnp.float32)
    process = jnp.diag(noise_var)

    def forward(carry, item):
        mean, cov, index = carry
        step_op, step_value, step_noise, step_block, step_count = item
        info, shift = step_information(step_op, step_value, step_noise, step_block, step_count, nblocks)
        first = index == 0
        pred_mean = jnp.where(first, prior_mean, product(transition, mean))
        pred_cov = jnp.where(first, jnp.diag(prior_var), product(product(transition, cov), transition.T) + process)
        factor = jnp.linalg.cholesky(pred_cov)
        pred_prec = jax.scipy.linalg.cho_solve((factor, True), eye)
        post_factor = jnp.linalg.cholesky(pred_prec + info)
        new_cov = jax.scipy.linalg.cho_solve((post_factor, True), eye)
        new_mean = product(new_cov, product(pred_prec, pred_mean) + shift)
        return ((new_mean, new_cov, index + 1), (new_mean, new_cov))
    start = (jnp.zeros((width,), jnp.float32), eye, jnp.zeros((), jnp.int32))
    _, (means, covs) = lax.scan(forward, start, (obs_op, obs_value, obs_noise, obs_block, obs_count))

    def backward(carry, item):
        next_mean, next_cov = carry
        mean, cov = item
        moved = product(transition, cov)
        predicted = product(moved, transition.T) + process
        factor = jnp.linalg.cholesky(predicted)
        gain = jax.scipy.linalg.cho_solve((factor, True), moved).T
        smooth_mean = mean + product(gain, next_mean - product(transition, mean))
        smooth_cov = cov + product(product(gain, next_cov - predicted), gain.T)
        return ((smooth_mean, smooth_cov), (smooth_mean, jnp.diagonal(smooth_cov)))
    _, (lower_mean, lower_var) = lax.scan(backward, (means[-1], covs[-1]), (means[:-1], covs[:-1]), reverse=True)
    smoothed_mean = jnp.concatenate([lower_mean, means[-1][None]], axis=0)
    smoothed_var = jnp.concatenate([lower_var, jnp.diagonal(covs[-1])[None]], axis=0)
    return (smoothed_mean, smoothed_var)
```

```python
import functools

import jax
import jax.numpy as jnp
from jax import lax
from jax.experimental import pallas as pl
from jax.experimental.pallas import tpu as pltpu
from jax.sharding import PartitionSpec as P

f32 = jnp.float32
bf16 = jnp.bfloat16


def halves(value):
    high = value.astype(bf16)
    return high, (value - high.astype(f32)).astype(bf16)


def mul_halves(left, right, contract):
    dims = (contract, ((), ()))
    a, b = left
    c, d = right
    out = lax.dot_general(a, d, dims, preferred_element_type=f32)
    out = out + lax.dot_general(b, c, dims, preferred_element_type=f32)
    return out + lax.dot_general(a, c, dims, preferred_element_type=f32)


def mul(left, right):
    return mul_halves(halves(left), halves(right), ((1,), (0,)))


def mul_nt(left, right):
    return mul_halves(halves(left), halves(right), ((1,), (1,)))


def masks(size):
    rows = lax.broadcasted_iota(jnp.int32, (size, size), 0)
    cols = lax.broadcasted_iota(jnp.int32, (size, size), 1)
    return rows > cols, rows == cols


def rows8(vector):
    return jnp.broadcast_to(vector, (8, vector.shape[1]))


def invert(m, work):
    size = m.shape[0]
    _, diag = masks(size)
    eye = diag.astype(f32)
    magnitude = jnp.abs(m)
    bound = jnp.minimum(
        jnp.max(jnp.sum(magnitude, axis=1, keepdims=True)),
        jnp.max(jnp.sum(magnitude, axis=0, keepdims=True)),
    )
    scale = 2.0 / (2.0 + bound)
    work[0:size] = scale * eye
    work[size : 2 * size] = (1.0 - scale) * eye - scale * m

    def more(radius):
        return radius > 1e-4

    def step(radius):
        square = radius * radius
        factor = 2.0 / (2.0 - square)
        whole = work[...]
        out = mul(whole, whole[size : 2 * size])
        work[0:size] = factor * (whole[0:size] + out[0:size])
        work[size : 2 * size] = factor * out[size : 2 * size] + (1.0 - factor) * eye
        return square / (2.0 - square)

    lax.while_loop(more, step, jnp.minimum(bound / (2.0 + bound), 1.0 - 1e-6))
    x = work[0:size]
    residual = eye - x - mul(x, m)
    return x + mul(residual, x)


def unpack(ref, size):
    below, diag = masks(size)
    linear = ref[0:size]
    square = ref[size : 2 * size]
    turned = square.T
    upto = jnp.logical_or(below, diag)
    info = jnp.where(upto, square, turned)
    cov = jnp.where(upto, turned, square)
    tail = ref[2 * size : 2 * size + 8]
    cov = jnp.where(diag, tail[2:3], cov)
    return linear, tail[0:1], cov, tail[1:2], info


def pack(ref, linear, offset, cov, vector, info):
    size = cov.shape[0]
    below, diag = masks(size)
    ref[0:size] = linear
    ref[size : 2 * size] = jnp.where(jnp.logical_or(below, diag), info, cov)
    diagonal = jnp.sum(jnp.where(diag, cov, 0.0), axis=0, keepdims=True)
    ref[2 * size : 2 * size + 8] = jnp.concatenate(
        [offset, vector, diagonal, jnp.zeros((5, size), f32)], axis=0
    )


def fold(first, second, work):
    lin1, off1, cov1, vec1, inf1 = first
    lin2, off2, cov2, vec2, inf2 = second
    size = cov1.shape[0]
    top = mul(jnp.concatenate([cov1, rows8(off1)], axis=0), inf2)
    pull = vec2 - top[size : size + 1]
    push = off1 + mul(rows8(vec2), cov1)[0:1]
    weight = invert(top[0:size], work)
    moved = mul_nt(rows8(push), weight)
    weight_lin = mul(weight, lin1)
    weight_cov = mul(weight, cov1)
    left = mul(jnp.concatenate([lin2, inf2, rows8(pull)], axis=0), weight_lin)
    linear = left[0:size]
    vector = vec1 + left[2 * size : 2 * size + 1]
    info = inf1 + mul(lin1.T, left[size : 2 * size])
    spread = mul(lin2, weight_cov)
    last = mul_nt(jnp.concatenate([spread, moved], axis=0), lin2)
    return linear, off2 + last[size : size + 1], cov2 + last[0:size], vector, info


def half_fold(cov1, off1, second, work):
    lin2, off2, cov2, vec2, inf2 = second
    size = cov1.shape[0]
    push = off1 + mul(rows8(vec2), cov1)[0:1]
    weight = invert(mul(cov1, inf2), work)
    moved = mul_nt(rows8(push), weight)
    spread = mul(lin2, mul(weight, cov1))
    last = mul_nt(jnp.concatenate([spread, moved], axis=0), lin2)
    return cov2 + last[0:size], off2 + last[size : size + 1]


def build_kernel(flags, trans, params, op_ref, val_ref, noise_ref, blocks, counts, out, info_ref, work):
    slots, stations, width = op_ref.shape
    size = trans.shape[0]
    step = flags[0]
    count = counts[0, 0]
    noise = noise_ref[...]
    noise_cols = noise.T
    weighted = val_ref[...] / noise
    info_ref[...] = jnp.zeros(info_ref.shape, f32)
    shifts = []
    for a in range(size // width):
        info = jnp.zeros((width, width), f32)
        shift = jnp.zeros((8, width), f32)
        for m in range(slots):
            keep = jnp.logical_and(m < count, blocks[0, m] == a).astype(f32)
            op = op_ref[m]
            wide = op.astype(f32)
            scaled = (wide / noise_cols[:, m : m + 1]).astype(bf16)
            part = lax.dot_general(
                scaled, op, (((0,), (0,)), ((), ())), preferred_element_type=f32
            )
            info = info + keep * part
            shift = shift + keep * jnp.dot(
                rows8(weighted[m : m + 1]),
                wide,
                precision=lax.Precision.HIGHEST,
                preferred_element_type=f32,
            )
        info = 0.5 * (info + info.T)
        info_ref[a * width : (a + 1) * width, a * width : (a + 1) * width] = info
        shifts.append(shift[0:1])
    h = jnp.concatenate(shifts, axis=1)
    info = info_ref[...]
    rows = params[...]
    first = (step == 0).astype(f32)
    var = first * rows[2:3] + (1.0 - first) * rows[0:1]
    mean = first * rows[1:2]
    moving = (1.0 - first) * trans[...]
    turned = invert(info * var, work)
    weight = turned.T
    cov = weight * var
    linear = mul(weight, moving)
    small = mul(rows8(h), jnp.concatenate([cov, linear], axis=1))
    offset = small[0:1, 0:size] + mul(rows8(mean), turned)[0:1]
    vector = small[0:1, size : 2 * size]
    info_moved = mul(moving.T, mul(info, linear))
    pack(out, linear, offset, cov, vector, info_moved)


def pair_kernel(flags, mine, other, out, work):
    size = mine.shape[1]
    core = flags[1]
    end = flags[2]
    swap = core == 1
    own = unpack(mine, size)
    far = unpack(other, size)
    first = [jnp.where(swap, b, a) for a, b in zip(own, far)]
    second = [jnp.where(swap, a, b) for a, b in zip(own, far)]
    keep = 1.0 - end.astype(f32)
    second = [second[0] * keep, second[1] * keep, second[2] * keep, second[3], second[4]]
    linear, offset, cov, vector, info = fold(first, second, work)
    pack(
        out,
        jnp.where(swap, linear.T, linear),
        jnp.where(swap, vector, offset),
        jnp.where(swap, info, cov),
        jnp.where(swap, -offset, vector),
        jnp.where(swap, cov, info),
    )


def fold_kernel(mine, received, out, work):
    size = mine.shape[1]
    pack(out, *fold(unpack(received, size), unpack(mine, size), work))


def put_half(out, cov, offset):
    size = cov.shape[0]
    out[0:size] = cov
    out[size : size + 8] = rows8(offset)


def half_kernel(mine, received, out, work):
    size = mine.shape[1]
    cov, offset = half_fold(
        received[0:size], received[size : size + 1], unpack(mine, size), work
    )
    put_half(out, cov, offset)


def own_half_kernel(flags, mine, received, out, work):
    size = mine.shape[1]
    swap = flags[1] == 1
    linear, offset, cov, vector, info = unpack(mine, size)
    second = (
        jnp.where(swap, linear.T, linear),
        jnp.where(swap, vector, offset),
        jnp.where(swap, info, cov),
        jnp.where(swap, -offset, vector),
        jnp.where(swap, cov, info),
    )
    cov, offset = half_fold(received[0:size], received[size : size + 1], second, work)
    put_half(out, cov, offset)


def finish_kernel(flags, prefix, suffix, mean_out, var_out, work):
    size = prefix.shape[1]
    cov = prefix[0:size]
    mean = prefix[size : size + 1]
    info = suffix[0:size]
    vector = suffix[size : size + 1]
    push = mean + mul(rows8(vector), cov)[0:1]
    weight = invert(mul(cov, info), work)
    mean_out[...] = mul_nt(rows8(push), weight)[0:1]
    _, diag = masks(size)
    var_out[...] = jnp.sum(jnp.where(diag, mul(weight, cov), 0.0), axis=0, keepdims=True)


def run(body, out_shapes, size, *args, scalars=0, extra=(), smem=()):
    vmem = pl.BlockSpec(memory_space=pltpu.VMEM)
    spaces = [
        pl.BlockSpec(memory_space=pltpu.SMEM) if index < scalars or index in smem else vmem
        for index in range(len(args))
    ]
    single = len(out_shapes) == 1
    shapes = [jax.ShapeDtypeStruct(shape, f32) for shape in out_shapes]
    return pl.pallas_call(
        body,
        out_shape=shapes[0] if single else shapes,
        in_specs=spaces,
        out_specs=vmem if single else [vmem] * len(shapes),
        scratch_shapes=list(extra) + [pltpu.VMEM((2 * size, size), f32)],
        compiler_params=pltpu.CompilerParams(vmem_limit_bytes=48 * 1024 * 1024),
        name=body.__name__,
    )(*args)


def local(
    transition, noise_var, prior_mean, prior_var, obs_op, obs_value, obs_noise, obs_block, obs_count
):
    size = transition.shape[0]
    devices = lax.axis_size("tm")
    pairs = devices // 2
    device = lax.axis_index("tm")
    core = device % 2
    flags = jnp.stack([device, core, (device >= devices - 2) * core, 0]).astype(jnp.int32)
    message = (2 * size + 8, size)
    half = (size + 8, size)
    params = jnp.concatenate(
        [noise_var[None], prior_mean[None], prior_var[None], jnp.zeros((5, size), f32)], axis=0
    )
    trade = [(d, d ^ 1) for d in range(devices)]

    def along(offset):
        ups = [(2 * c, 2 * (c + offset)) for c in range(pairs - offset)]
        downs = [(2 * (c + offset) + 1, 2 * c + 1) for c in range(pairs - offset)]
        return ups + downs

    element = run(
        build_kernel,
        [message],
        size,
        flags,
        transition,
        params,
        obs_op[0],
        obs_value[0],
        obs_noise[0],
        obs_block,
        obs_count[None],
        scalars=1,
        smem=(6, 7),
        extra=[pltpu.VMEM((size, size), f32)],
    )
    other = lax.ppermute(element, "tm", trade)
    state = run(pair_kernel, [message], size, flags, element, other, scalars=1)
    offset = 1
    while 2 * offset < pairs:
        received = lax.ppermute(state, "tm", along(offset))
        state = run(fold_kernel, [message], size, state, received)
        offset *= 2

    def half_of(message_value):
        square = message_value[size : 2 * size]
        tail = message_value[2 * size :]
        upper = jnp.triu(square, 1)
        cov = upper + upper.T + jnp.diag(tail[2])
        return jnp.concatenate([cov, tail], axis=0)

    received = lax.ppermute(half_of(state), "tm", along(offset))
    whole = run(half_kernel, [half], size, state, received)
    before = lax.ppermute(whole, "tm", along(1))
    step = run(own_half_kernel, [half], size, flags, element, before, scalars=1)
    sent = jnp.where(core == 0, whole, step)
    got = lax.ppermute(sent, "tm", trade)
    prefix = jnp.where(core == 0, step, got)
    suffix = jnp.where(core == 0, got, before)
    mean, var = run(
        finish_kernel, [(1, size), (1, size)], size, flags, prefix, suffix, scalars=1
    )
    return mean, var


def solution(mesh):
    return jax.shard_map(
        local,
        mesh=mesh,
        in_specs=(
            P(),
            P(),
            P(),
            P(),
            P("tm", None, None, None),
            P("tm", None, None),
            P("tm", None, None),
            P("tm", None),
            P("tm"),
        ),
        out_specs=(P("tm", None), P("tm", None)),
        check_vma=False,
    )
```

```python
import functools

import jax
import jax.numpy as jnp
from jax import lax
from jax.experimental import pallas as pl
from jax.experimental.pallas import tpu as pltpu
from jax.sharding import PartitionSpec as P

f32 = jnp.float32
bf16 = jnp.bfloat16


def halves(value):
    high = value.astype(bf16)
    return high, (value - high.astype(f32)).astype(bf16)


def mul_halves(left, right, contract):
    dims = (contract, ((), ()))
    a, b = left
    c, d = right
    out = lax.dot_general(a, d, dims, preferred_element_type=f32)
    out = out + lax.dot_general(b, c, dims, preferred_element_type=f32)
    return out + lax.dot_general(a, c, dims, preferred_element_type=f32)


def mul(left, right):
    return mul_halves(halves(left), halves(right), ((1,), (0,)))


def mul_nt(left, right):
    return mul_halves(halves(left), halves(right), ((1,), (1,)))


def masks(size):
    rows = lax.broadcasted_iota(jnp.int32, (size, size), 0)
    cols = lax.broadcasted_iota(jnp.int32, (size, size), 1)
    return rows > cols, rows == cols


def rows8(vector):
    return jnp.broadcast_to(vector, (8, vector.shape[1]))


def invert(m, work):
    size = m.shape[0]
    _, diag = masks(size)
    eye = diag.astype(f32)
    magnitude = jnp.abs(m)
    bound = jnp.minimum(
        jnp.max(jnp.sum(magnitude, axis=1, keepdims=True)),
        jnp.max(jnp.sum(magnitude, axis=0, keepdims=True)),
    )
    scale = 2.0 / (2.0 + bound)
    work[0:size] = scale * eye
    work[size : 2 * size] = (1.0 - scale) * eye - scale * m

    def more(radius):
        return radius > 1e-4

    def step(radius):
        square = radius * radius
        factor = 2.0 / (2.0 - square)
        whole = work[...]
        out = mul(whole, whole[size : 2 * size])
        work[0:size] = factor * (whole[0:size] + out[0:size])
        work[size : 2 * size] = factor * out[size : 2 * size] + (1.0 - factor) * eye
        return square / (2.0 - square)

    lax.while_loop(more, step, jnp.minimum(bound / (2.0 + bound), 1.0 - 1e-6))
    x = work[0:size]
    residual = eye - x - mul(x, m)
    return x + mul(residual, x)


def unpack(tail, linear, square):
    below, diag = masks(square.shape[0])
    turned = square.T
    upto = jnp.logical_or(below, diag)
    info = jnp.where(upto, square, turned)
    cov = jnp.where(upto, turned, square)
    cov = jnp.where(diag, tail[2:3], cov)
    return linear, tail[0:1], cov, tail[1:2], info


def unpack_whole(ref):
    size = ref.shape[1]
    return unpack(ref[0:8], ref[8 : size + 8], ref[size + 8 : 2 * size + 8])


def unpack_halves(got, far, core):
    size = got.shape[1]
    swap = core == 1
    own = got[...]
    other = far[...]
    head = jnp.where(swap, other, own)
    square = jnp.where(swap, own[8:], other[8:])
    return unpack(head[0:8], head[8:], square)


def dual(flag, element):
    linear, offset, cov, vector, info = element
    return (
        jnp.where(flag, linear.T, linear),
        jnp.where(flag, vector, offset),
        jnp.where(flag, info, cov),
        jnp.where(flag, -offset, vector),
        jnp.where(flag, cov, info),
    )


def ordered(flag, one, two):
    return (
        [jnp.where(flag, b, a) for a, b in zip(one, two)],
        [jnp.where(flag, a, b) for a, b in zip(one, two)],
    )


def pack(linear, offset, cov, vector, info):
    size = cov.shape[0]
    below, diag = masks(size)
    square = jnp.where(jnp.logical_or(below, diag), info, cov)
    diagonal = jnp.sum(jnp.where(diag, cov, 0.0), axis=0, keepdims=True)
    tail = jnp.concatenate([offset, vector, diagonal, jnp.zeros((5, size), f32)], axis=0)
    return jnp.concatenate([tail, linear, square], axis=0)


def fold(first, second, work):
    lin1, off1, cov1, vec1, inf1 = first
    lin2, off2, cov2, vec2, inf2 = second
    size = cov1.shape[0]
    top = mul(jnp.concatenate([cov1, rows8(off1)], axis=0), inf2)
    pull = vec2 - top[size : size + 1]
    push = off1 + mul(rows8(vec2), cov1)[0:1]
    weight = invert(top[0:size], work)
    moved = mul_nt(rows8(push), weight)
    weight_lin = mul(weight, lin1)
    weight_cov = mul(weight, cov1)
    left = mul(jnp.concatenate([lin2, inf2, rows8(pull)], axis=0), weight_lin)
    linear = left[0:size]
    vector = vec1 + left[2 * size : 2 * size + 1]
    info = inf1 + mul(lin1.T, left[size : 2 * size])
    spread = mul(lin2, weight_cov)
    last = mul_nt(jnp.concatenate([spread, moved], axis=0), lin2)
    return linear, off2 + last[size : size + 1], cov2 + last[0:size], vector, info


def half_fold(cov1, off1, second, work):
    lin2, off2, cov2, vec2, inf2 = second
    size = cov1.shape[0]
    push = off1 + mul(rows8(vec2), cov1)[0:1]
    weight = invert(mul(cov1, inf2), work)
    moved = mul_nt(rows8(push), weight)
    spread = mul(lin2, mul(weight, cov1))
    last = mul_nt(jnp.concatenate([spread, moved], axis=0), lin2)
    return cov2 + last[0:size], off2 + last[size : size + 1]


def build_kernel(
    flags, trans_in, params_in, op_in, val_in, noise_in, blocks_in, counts_in, out,
    trans, params, op_ref, val_ref, noise_ref, blocks, counts, sems, info_ref, work,
):
    pairs = (
        (op_in, op_ref), (noise_in, noise_ref), (val_in, val_ref), (blocks_in, blocks),
        (counts_in, counts), (params_in, params), (trans_in, trans),
    )
    copies = [
        pltpu.make_async_copy(source, target, sems.at[index])
        for index, (source, target) in enumerate(pairs)
    ]
    for copy in copies:
        copy.start()
    for copy in copies[:5]:
        copy.wait()
    slots, stations, width = op_ref.shape
    size = trans.shape[0]
    step = flags[0]
    count = counts[0, 0]
    noise = noise_ref[...]
    noise_cols = noise.T
    weighted = val_ref[...] / noise
    info_ref[...] = jnp.zeros(info_ref.shape, f32)
    shifts = []
    for a in range(size // width):
        info = jnp.zeros((width, width), f32)
        shift = jnp.zeros((8, width), f32)
        for m in range(slots):
            keep = jnp.logical_and(m < count, blocks[0, m] == a).astype(f32)
            op = op_ref[m]
            wide = op.astype(f32)
            scaled = (wide / noise_cols[:, m : m + 1]).astype(bf16)
            part = lax.dot_general(
                scaled, op, (((0,), (0,)), ((), ())), preferred_element_type=f32
            )
            info = info + keep * part
            shift = shift + keep * jnp.dot(
                rows8(weighted[m : m + 1]),
                wide,
                precision=lax.Precision.HIGHEST,
                preferred_element_type=f32,
            )
        info = 0.5 * (info + info.T)
        info_ref[a * width : (a + 1) * width, a * width : (a + 1) * width] = info
        shifts.append(shift[0:1])
    h = jnp.concatenate(shifts, axis=1)
    info = info_ref[...]
    for copy in copies[5:]:
        copy.wait()
    rows = params[...]
    first = (step == 0).astype(f32)
    var = first * rows[2:3] + (1.0 - first) * rows[0:1]
    mean = first * rows[1:2]
    moving = (1.0 - first) * trans[...]
    turned = invert(info * var, work)
    weight = turned.T
    cov = weight * var
    linear = mul(weight, moving)
    small = mul(rows8(h), jnp.concatenate([cov, linear], axis=1))
    offset = small[0:1, 0:size] + mul(rows8(mean), turned)[0:1]
    vector = small[0:1, size : 2 * size]
    info_moved = mul(moving.T, mul(info, linear))
    out[...] = pack(linear, offset, cov, vector, info_moved)


def put_sent(out, sent, core):
    size = out.shape[1]
    sent[...] = out[pl.ds(core * size, size + 8)]


def put_edge(cov, offset, sent):
    size = cov.shape[0]
    sent[0:8] = rows8(offset)
    sent[8 : size + 8] = cov


def pair_kernel(flags, mine, other, sent, sides, work):
    size = mine.shape[1]
    core = flags[1]
    high = core == 1
    own = unpack_whole(mine)
    far = unpack_whole(other)
    whole = pack(*fold(*ordered(high, own, far), work))
    sides[2] = whole
    put_sent(sides.at[2], sent, core)
    _, diag = masks(size)
    eye = diag.astype(f32)
    none = jnp.zeros((8, size), f32)
    neutral = jnp.concatenate([none, eye, jnp.zeros((size, size), f32)], axis=0)
    sides[1] = jnp.where(high, whole, mine[...])
    sides[0] = jnp.where(high, neutral, pack(*dual(jnp.logical_not(high), far)))


def fold_kernel(flags, bits, sides, got, far, out, sent, work):
    core = flags[1]
    high = bits[0] == 1
    received = unpack_halves(got, far, core)
    out[...] = pack(*fold(*ordered(high, unpack_whole(sides.at[2]), received), work))
    put_sent(out, sent, core)


def edge_kernel(flags, bits, sides, got, far, sent, work):
    core = flags[1]
    high = bits[0] == 1
    received = unpack_halves(got, far, core)
    _, offset, cov, vector, info = fold(
        *ordered(high, unpack_whole(sides.at[2]), received), work
    )
    upper = bits[1] == 1
    put_edge(jnp.where(upper, info, cov), jnp.where(upper, vector, offset), sent)


def side_kernel(flags, bits, sides, state, got, far, out, work):
    core = flags[1]
    bit = bits[0]
    received = dual(bit == 0, unpack_halves(got, far, core))
    out[1 - bit] = sides[1 - bit]
    out[2] = state[...]
    out[bit] = pack(*fold(received, unpack_whole(sides.at[bit]), work))


def close_kernel(flags, bits, sides, got, far, out, work):
    size = got.shape[1]
    core = flags[1]
    bit = bits[0]
    upper = bits[1] == 1
    received = dual(bit == 0, unpack_halves(got, far, core))
    fresh = fold(received, unpack_whole(sides.at[bit]), work)
    kept = unpack_whole(sides.at[1 - bit])
    back, front = ordered(bit == 1, fresh, kept)
    _, diag = masks(size)
    eye = diag.astype(f32)
    back_lin, back_off, back_cov, back_vec, back_inf = back
    front_lin, mean, cov, front_vec, front_inf = front
    none = jnp.zeros((1, size), f32)
    zero = jnp.zeros((size, size), f32)
    first = (
        jnp.where(upper, front_lin, cov),
        mean,
        cov,
        jnp.where(upper, front_vec, none),
        jnp.where(upper, front_inf, zero),
    )
    second = (
        jnp.where(upper, eye, back_lin.T),
        jnp.where(upper, none, -back_vec),
        jnp.where(upper, zero, back_inf),
        back_off,
        back_cov,
    )
    linear, offset, spread, vector, info = fold(first, second, work)
    base = jnp.where(upper, spread, cov - info)
    base = jnp.sum(jnp.where(diag, base, 0.0), axis=0, keepdims=True)
    out[0:8] = jnp.concatenate(
        [
            jnp.where(upper, vector, -offset),
            jnp.where(upper, offset, mean + vector),
            base,
            jnp.zeros((5, size), f32),
        ],
        axis=0,
    )
    out[8 : size + 8] = jnp.where(upper, linear.T, linear)
    out[size + 8 : 2 * size + 8] = jnp.where(upper, info, spread)


def last_kernel(flags, bits, closed, received, mean_out, var_out, work):
    size = received.shape[1]
    sign = (2 * bits[1] - 1).astype(f32)
    matrix = received[8 : size + 8]
    rows = closed[0:8]
    turned = closed[8 : size + 8]
    spread = mul(matrix, turned)
    push = received[0:1] + mul(rows8(rows[0:1]), matrix)[0:1]
    weight = invert(mul(matrix, closed[size + 8 : 2 * size + 8]), work)
    moved = mul_nt(rows8(push), weight)
    mean_out[...] = rows[1:2] + mul(moved, turned)[0:1]
    var_out[...] = rows[2:3] + sign * jnp.sum(
        turned * mul(weight, spread), axis=0, keepdims=True
    )


def run(body, out_shapes, size, *args, scalars=0, extra=(), raw=False):
    vmem = pl.BlockSpec(memory_space=pltpu.VMEM)
    rest = pl.BlockSpec(memory_space=pltpu.HBM) if raw else vmem
    spaces = [
        pl.BlockSpec(memory_space=pltpu.SMEM) if index < scalars else rest
        for index in range(len(args))
    ]
    single = len(out_shapes) == 1
    shapes = [jax.ShapeDtypeStruct(shape, f32) for shape in out_shapes]
    return pl.pallas_call(
        body,
        out_shape=shapes[0] if single else shapes,
        in_specs=spaces,
        out_specs=vmem if single else [vmem] * len(shapes),
        scratch_shapes=list(extra) + [pltpu.VMEM((2 * size, size), f32)],
        compiler_params=pltpu.CompilerParams(vmem_limit_bytes=16 * 1024 * 1024),
        name=body.__name__,
    )(*args)


def local(
    transition, noise_var, prior_mean, prior_var, obs_op, obs_value, obs_noise, obs_block, obs_count
):
    size = transition.shape[0]
    devices = lax.axis_size("tm")
    levels = (devices - 1).bit_length()
    device = lax.axis_index("tm")
    core = device % 2
    flags = jnp.stack([device, core]).astype(jnp.int32)
    message = (2 * size + 8, size)
    half = (size + 8, size)
    params = jnp.concatenate(
        [noise_var[None], prior_mean[None], prior_var[None], jnp.zeros((5, size), f32)], axis=0
    )
    _, slots, stations, width = obs_op.shape

    def traded(value, level):
        return lax.ppermute(value, "tm", [(d, d ^ (1 << level)) for d in range(devices)])

    element = run(
        build_kernel,
        [message],
        size,
        flags,
        transition,
        params,
        obs_op[0],
        obs_value[0],
        obs_noise[0],
        obs_block,
        obs_count[None],
        scalars=1,
        raw=True,
        extra=[
            pltpu.VMEM((size, size), f32),
            pltpu.VMEM((8, size), f32),
            pltpu.VMEM((slots, stations, width), bf16),
            pltpu.VMEM((slots, stations), f32),
            pltpu.VMEM((slots, stations), f32),
            pltpu.SMEM((1, slots), jnp.int32),
            pltpu.SMEM((1, 1), jnp.int32),
            pltpu.SemaphoreType.DMA((7,)),
            pltpu.VMEM((size, size), f32),
        ],
    )
    other = traded(element, 0)
    sent, sides = run(
        pair_kernel, [half, (3,) + message], size, flags, element, other, scalars=1
    )
    for level in range(1, levels - 1):
        bits = jnp.stack([(device >> level) % 2, (device >> (level + 1)) % 2]).astype(jnp.int32)
        got = traded(sent, level)
        got, sides = lax.optimization_barrier((got, sides))
        far = traded(got, 0)
        if level < levels - 2:
            state, sent = run(
                fold_kernel, [message, half], size, flags, bits, sides, got, far, scalars=2
            )
            sides = run(
                side_kernel,
                [(3,) + message],
                size,
                flags,
                bits,
                sides,
                state,
                got,
                far,
                scalars=2,
            )
        else:
            sent = run(edge_kernel, [half], size, flags, bits, sides, got, far, scalars=2)
            _, held = lax.optimization_barrier((sent, sides))
            closed = run(close_kernel, [message], size, flags, bits, held, got, far, scalars=2)
    received = traded(sent, levels - 1)
    mean, var = run(
        last_kernel, [(1, size), (1, size)], size, flags, bits, closed, received, scalars=2
    )
    return mean, var


def solution(mesh):
    return jax.shard_map(
        local,
        mesh=mesh,
        in_specs=(
            P(),
            P(),
            P(),
            P(),
            P("tm", None, None, None),
            P("tm", None, None),
            P("tm", None, None),
            P("tm", None),
            P("tm"),
        ),
        out_specs=(P("tm", None), P("tm", None)),
        check_vma=False,
    )
```

```python
import functools

import jax
import jax.numpy as jnp
from jax import lax
from jax.experimental import pallas as pl
from jax.experimental.pallas import tpu as pltpu
from jax.sharding import PartitionSpec as P

f32 = jnp.float32
bf16 = jnp.bfloat16


def halves(value):
    high = value.astype(bf16)
    return high, (value - high.astype(f32)).astype(bf16)


ROWS = ((1,), (0,))
TURNED = ((1,), (1,))


def mul_halves(left, right, contract=ROWS):
    dims = (contract, ((), ()))
    a, b = left
    c, d = right
    rows = a.shape[0]
    both = lax.dot_general(jnp.concatenate([a, b], axis=0), c, dims, preferred_element_type=f32)
    return both[0:rows] + (both[rows:] + lax.dot_general(a, d, dims, preferred_element_type=f32))


def mul(left, right):
    return mul_halves(halves(left), halves(right))


def mul_nt(left, right):
    return mul_halves(halves(left), halves(right), TURNED)


def stack(*parts):
    return tuple(jnp.concatenate(group, axis=0) for group in zip(*parts))


def masks(size):
    rows = lax.broadcasted_iota(jnp.int32, (size, size), 0)
    cols = lax.broadcasted_iota(jnp.int32, (size, size), 1)
    return rows > cols, rows == cols


def rows8(vector):
    return jnp.broadcast_to(vector, (8, vector.shape[1]))


def invert(m, work):
    size = m.shape[0]
    _, diag = masks(size)
    eye = diag.astype(f32)
    magnitude = jnp.abs(m)
    bound = jnp.minimum(
        jnp.max(jnp.sum(magnitude, axis=1, keepdims=True)),
        jnp.max(jnp.sum(magnitude, axis=0, keepdims=True)),
    )
    scale = 2.0 / (2.0 + bound)
    work[0:size] = scale * eye
    work[size : 2 * size] = (1.0 - scale) * eye - scale * m

    def step(radius):
        square = radius * radius
        factor = 2.0 / (2.0 - square)
        whole = work[...]
        low = whole.astype(bf16)
        out = jnp.dot(low, low[size : 2 * size], preferred_element_type=f32)
        work[0:size] = factor * (whole[0:size] + out[0:size])
        work[size : 2 * size] = factor * out[size : 2 * size] + (1.0 - factor) * eye
        return square / (2.0 - square)

    lax.while_loop(
        lambda radius: radius > 1e-2, step, jnp.minimum(bound / (2.0 + bound), 1.0 - 1e-6)
    )
    split = halves(m)

    def more(carry):
        square_of, count = carry
        return jnp.logical_and(square_of > 2e-3, count < 60)

    def correct(carry):
        _, count = carry
        x = work[0:size]
        x_halves = halves(x)
        residual = eye - x - mul_halves(x_halves, split)
        low = residual.astype(bf16)
        square = jnp.dot(low, low, preferred_element_type=f32)
        square_of = jnp.max(jnp.sum(jnp.abs(square), axis=0, keepdims=True))
        bad = jnp.logical_and(count == 0, jnp.logical_not(square_of < 0.25))
        better = x + mul_halves(halves(residual + square), x_halves)
        work[0:size] = jnp.where(bad, scale * eye, better)
        return jnp.where(bad, 1.0, square_of), count + 1

    lax.while_loop(more, correct, (jnp.float32(1.0), jnp.int32(0)))
    return work[0:size]


def unpack(tail, linear, square):
    below, diag = masks(square.shape[0])
    turned = square.T
    upto = jnp.logical_or(below, diag)
    info = jnp.where(upto, square, turned)
    cov = jnp.where(upto, turned, square)
    cov = jnp.where(diag, tail[2:3], cov)
    return linear, tail[0:1], cov, tail[1:2], info


def unpack_whole(ref):
    size = ref.shape[1]
    return unpack(ref[0:8], ref[8 : size + 8], ref[size + 8 : 2 * size + 8])


def unpack_halves(got, far, core):
    size = got.shape[1]
    swap = core == 1
    own = got[...]
    other = far[...]
    head = jnp.where(swap, other, own)
    square = jnp.where(swap, own[8:], other[8:])
    return unpack(head[0:8], head[8:], square)


def dual(flag, element):
    linear, offset, cov, vector, info = element
    return (
        jnp.where(flag, linear.T, linear),
        jnp.where(flag, vector, offset),
        jnp.where(flag, info, cov),
        jnp.where(flag, -offset, vector),
        jnp.where(flag, cov, info),
    )


def ordered(flag, one, two):
    return (
        [jnp.where(flag, b, a) for a, b in zip(one, two)],
        [jnp.where(flag, a, b) for a, b in zip(one, two)],
    )


def pack(linear, offset, cov, vector, info):
    size = cov.shape[0]
    below, diag = masks(size)
    square = jnp.where(jnp.logical_or(below, diag), info, cov)
    diagonal = jnp.sum(jnp.where(diag, cov, 0.0), axis=0, keepdims=True)
    tail = jnp.concatenate([offset, vector, diagonal, jnp.zeros((5, size), f32)], axis=0)
    return jnp.concatenate([tail, linear, square], axis=0)


def fold(first, second, work):
    lin1, off1, cov1, vec1, inf1 = first
    lin2, off2, cov2, vec2, inf2 = second
    size = cov1.shape[0]
    cov1_halves = halves(cov1)
    lin1_halves = halves(lin1)
    lin2_halves = halves(lin2)
    inf2_halves = halves(inf2)
    top = mul_halves(stack(cov1_halves, halves(rows8(off1))), inf2_halves)
    pull = halves(rows8(vec2 - top[size : size + 1]))
    weight = halves(invert(top[0:size], work[0]))
    moved = halves(mul_halves(stack(lin2_halves, inf2_halves, pull), weight))
    lin_halves = tuple(part[0:size] for part in moved)
    left = mul_halves(moved, lin1_halves)
    spread = mul_halves(stack(lin_halves, halves(rows8(vec2))), cov1_halves)
    push = off1 + spread[size : size + 1]
    info = inf1 + mul(lin1.T, left[size : 2 * size])
    cov = cov2 + mul_halves(halves(spread[0:size]), lin2_halves, TURNED)
    offset = off2 + mul_halves(halves(rows8(push)), lin_halves, TURNED)[0:1]
    return left[0:size], offset, cov, vec1 + left[2 * size : 2 * size + 1], info


def half_fold(cov1, off1, second, work):
    lin2, off2, cov2, vec2, inf2 = second
    size = cov1.shape[0]
    cov1_halves = halves(cov1)
    lin2_halves = halves(lin2)
    weight = invert(mul_halves(cov1_halves, halves(inf2)), work[0])
    lin_halves = halves(mul_halves(lin2_halves, halves(weight)))
    spread = mul_halves(stack(lin_halves, halves(rows8(vec2))), cov1_halves)
    push = off1 + spread[size : size + 1]
    cov = cov2 + mul_halves(halves(spread[0:size]), lin2_halves, TURNED)
    offset = off2 + mul_halves(halves(rows8(push)), lin_halves, TURNED)[0:1]
    return cov, offset


def build_kernel(flags, trans, op_ref, rows, out, info_ref, work):
    slots, stations, width = op_ref.shape
    size = trans.shape[0]
    step = flags[0]
    value = rows[0:slots]
    noise = rows[slots : 2 * slots]

    def row(index):
        at = 2 * slots + 2 * index
        return jnp.concatenate([rows[at : at + 1], rows[at + 1 : at + 2]], axis=1)

    var_row, mean_row, start_row = row(0), row(1), row(2)
    count = rows[2 * slots + 6 : 2 * slots + 7, 0:1]
    blocks = rows[2 * slots + 7 : 2 * slots + 8]
    noise_cols = noise.T
    weighted = value / noise
    info_ref[...] = jnp.zeros(info_ref.shape, f32)
    shifts = []
    for a in range(size // width):
        info = jnp.zeros((width, width), f32)
        shift = jnp.zeros((8, width), f32)
        for m in range(slots):
            keep = jnp.logical_and(count > m, blocks[:, m : m + 1] == a).astype(f32)
            op = op_ref[m]
            wide = op.astype(f32)
            scaled = (wide / noise_cols[:, m : m + 1]).astype(bf16)
            part = lax.dot_general(
                scaled, op, (((0,), (0,)), ((), ())), preferred_element_type=f32
            )
            info = info + keep * part
            shift = shift + keep * jnp.dot(
                rows8(weighted[m : m + 1]),
                wide,
                precision=lax.Precision.HIGHEST,
                preferred_element_type=f32,
            )
        info = 0.5 * (info + info.T)
        info_ref[a * width : (a + 1) * width, a * width : (a + 1) * width] = info
        shifts.append(shift[0:1])
    h = jnp.concatenate(shifts, axis=1)
    info = info_ref[...]
    first = (step == 0).astype(f32)
    var = first * start_row + (1.0 - first) * var_row
    mean = first * mean_row
    moving = (1.0 - first) * trans[...]
    turned = invert(info * var, work)
    weight = turned.T
    cov = weight * var
    linear = mul(weight, moving)
    small = mul(rows8(h), jnp.concatenate([cov, linear], axis=1))
    offset = small[0:1, 0:size] + mul(rows8(mean), turned)[0:1]
    vector = small[0:1, size : 2 * size]
    info_moved = mul(moving.T, mul(info, linear))
    out[...] = pack(linear, offset, cov, vector, info_moved)


def put_sent(out, sent, core):
    size = out.shape[1]
    sent[...] = out[pl.ds(core * size, size + 8)]


def put_edge(cov, offset, sent):
    size = cov.shape[0]
    sent[0:8] = rows8(offset)
    sent[8 : size + 8] = cov


def pair_kernel(flags, mine, other, state, sent, sides, *work):
    size = mine.shape[1]
    core = flags[1]
    high = core == 1
    own = unpack_whole(mine)
    far = unpack_whole(other)
    whole = pack(*fold(*ordered(high, own, far), work))
    state[...] = whole
    put_sent(state, sent, core)
    _, diag = masks(size)
    eye = diag.astype(f32)
    none = jnp.zeros((8, size), f32)
    neutral = jnp.concatenate([none, eye, jnp.zeros((size, size), f32)], axis=0)
    sides[1] = jnp.where(high, whole, mine[...])
    sides[0] = jnp.where(high, neutral, pack(*dual(jnp.logical_not(high), far)))


def fold_kernel(flags, bits, state, got, far, out, sent, *work):
    core = flags[1]
    high = bits[0] == 1
    received = unpack_halves(got, far, core)
    out[...] = pack(*fold(*ordered(high, unpack_whole(out), received), work))
    put_sent(out, sent, core)


def edge_kernel(flags, bits, state, got, far, sent, *work):
    core = flags[1]
    high = bits[0] == 1
    upper = bits[1] == 1
    first, second = ordered(
        jnp.logical_xor(high, upper), unpack_whole(state), unpack_halves(got, far, core)
    )
    _, offset, cov, _, _ = dual(upper, first)
    cov, offset = half_fold(cov, offset, dual(upper, second), work)
    put_edge(cov, offset, sent)


def side_kernel(flags, bits, sides, got, far, out, *work):
    core = flags[1]
    bit = bits[0]
    received = dual(bit == 0, unpack_halves(got, far, core))
    out[bit] = pack(*fold(received, unpack_whole(out.at[bit]), work))


def close_kernel(flags, bits, sides, got, far, out, one, two, three, *work):
    size = got.shape[1]
    core = flags[1]
    bit = bits[0]
    upper = bits[1] == 1
    _, diag = masks(size)
    one[...] = pack(*dual(bit == 0, unpack_halves(got, far, core)))
    two[...] = sides[bit]

    def turn(index, carry):
        three[...] = pack(*fold(unpack_whole(one), unpack_whole(two), work))

        @pl.when(index == 0)
        def _():
            fresh = unpack_whole(three)
            kept = unpack_whole(sides.at[1 - bit])
            back, front = ordered(bit == 1, fresh, kept)
            eye = diag.astype(f32)
            back_lin, back_off, back_cov, back_vec, back_inf = back
            front_lin, mean, cov, front_vec, front_inf = front
            none = jnp.zeros((1, size), f32)
            zero = jnp.zeros((size, size), f32)
            one[...] = pack(
                jnp.where(upper, front_lin, cov),
                mean,
                cov,
                jnp.where(upper, front_vec, none),
                jnp.where(upper, front_inf, zero),
            )
            two[...] = pack(
                jnp.where(upper, eye, back_lin.T),
                jnp.where(upper, none, -back_vec),
                jnp.where(upper, zero, back_inf),
                back_off,
                back_cov,
            )

        return carry

    lax.fori_loop(0, 2, turn, 0)
    linear, offset, spread, vector, info = unpack_whole(three)
    _, mean, cov, _, _ = unpack_whole(one)
    base = jnp.where(upper, spread, cov - info)
    base = jnp.sum(jnp.where(diag, base, 0.0), axis=0, keepdims=True)
    out[0:8] = jnp.concatenate(
        [
            jnp.where(upper, vector, -offset),
            jnp.where(upper, offset, mean + vector),
            base,
            jnp.zeros((5, size), f32),
        ],
        axis=0,
    )
    out[8 : size + 8] = jnp.where(upper, linear.T, linear)
    out[size + 8 : 2 * size + 8] = jnp.where(upper, info, spread)


def last_kernel(flags, bits, closed, received, mean_out, var_out, work):
    size = received.shape[1]
    sign = (2 * bits[1] - 1).astype(f32)
    matrix = received[8 : size + 8]
    rows = closed[0:8]
    turned = closed[8 : size + 8]
    spread = mul(matrix, turned)
    push = received[0:1] + mul(rows8(rows[0:1]), matrix)[0:1]
    weight = invert(mul(matrix, closed[size + 8 : 2 * size + 8]), work)
    moved = mul_nt(rows8(push), weight)
    mean_out[...] = rows[1:2] + mul(moved, turned)[0:1]
    var_out[...] = rows[2:3] + sign * jnp.sum(
        turned * mul(weight, spread), axis=0, keepdims=True
    )


def run(body, out_shapes, size, *args, scalars=0, extra=(), aliases={}):
    vmem = pl.BlockSpec(memory_space=pltpu.VMEM)
    spaces = [
        pl.BlockSpec(memory_space=pltpu.SMEM) if index < scalars else vmem
        for index in range(len(args))
    ]
    single = len(out_shapes) == 1
    shapes = [jax.ShapeDtypeStruct(shape, f32) for shape in out_shapes]
    return pl.pallas_call(
        body,
        out_shape=shapes[0] if single else shapes,
        in_specs=spaces,
        out_specs=vmem if single else [vmem] * len(shapes),
        scratch_shapes=list(extra),
        input_output_aliases=aliases,
        compiler_params=pltpu.CompilerParams(vmem_limit_bytes=16 * 1024 * 1024),
        name=body.__name__,
    )(*args)


def local(
    transition, noise_var, prior_mean, prior_var, obs_op, obs_value, obs_noise, obs_block, obs_count
):
    size = transition.shape[0]
    devices = lax.axis_size("tm")
    levels = (devices - 1).bit_length()
    device = lax.axis_index("tm")
    core = device % 2
    flags = jnp.stack([device, core]).astype(jnp.int32)
    _, slots, stations, width = obs_op.shape
    assert size == 2 * stations
    rows = jnp.concatenate(
        [
            obs_value[0],
            obs_noise[0],
            noise_var.reshape(2, stations),
            prior_mean.reshape(2, stations),
            prior_var.reshape(2, stations),
            jnp.broadcast_to(obs_count[:, None].astype(f32), (1, stations)),
            jnp.pad(obs_block.astype(f32), ((0, 0), (0, stations - slots))),
        ],
        axis=0,
    )
    message = (2 * size + 8, size)
    half = (size + 8, size)
    inverse_work = [pltpu.VMEM((2 * size, size), f32)]

    def traded(value, level):
        return lax.ppermute(value, "tm", [(d, d ^ (1 << level)) for d in range(devices)])

    element = run(
        build_kernel,
        [message],
        size,
        flags,
        transition,
        obs_op[0],
        rows,
        scalars=1,
        extra=[pltpu.VMEM((size, size), f32)] + inverse_work,
    )
    other = traded(element, 0)
    state, sent, sides = run(
        pair_kernel,
        [message, half, (2,) + message],
        size,
        flags,
        element,
        other,
        scalars=1,
        extra=inverse_work,
    )
    for level in range(1, levels - 1):
        bits = jnp.stack([(device >> level) % 2, (device >> (level + 1)) % 2]).astype(jnp.int32)
        got = traded(sent, level)
        got, sides = lax.optimization_barrier((got, sides))
        far = traded(got, 0)
        now = (flags, bits, state, got, far)
        if level < levels - 2:
            state, sent = run(
                fold_kernel,
                [message, half],
                size,
                *now,
                scalars=2,
                extra=inverse_work,
                aliases={2: 0},
            )
        else:
            sent = run(edge_kernel, [half], size, *now, scalars=2, extra=inverse_work)
        _, sides = lax.optimization_barrier((sent, sides))
        now = (flags, bits, sides, got, far)
        if level < levels - 2:
            sides = run(
                side_kernel,
                [(2,) + message],
                size,
                *now,
                scalars=2,
                extra=inverse_work,
                aliases={2: 0},
            )
        else:
            closed = run(
                close_kernel,
                [message],
                size,
                *now,
                scalars=2,
                extra=[pltpu.VMEM(message, f32)] * 3 + inverse_work,
            )
    received = traded(sent, levels - 1)
    mean, var = run(
        last_kernel,
        [(1, size), (1, size)],
        size,
        flags,
        bits,
        closed,
        received,
        scalars=2,
        extra=inverse_work,
    )
    return mean, var


def solution(mesh):
    return jax.shard_map(
        local,
        mesh=mesh,
        in_specs=(
            P(),
            P(),
            P(),
            P(),
            P("tm", None, None, None),
            P("tm", None, None),
            P("tm", None, None),
            P("tm", None),
            P("tm"),
        ),
        out_specs=(P("tm", None), P("tm", None)),
        check_vma=False,
    )
```

```python
import functools

import jax
import jax.numpy as jnp
from jax import lax
from jax.experimental import pallas as pl
from jax.experimental.pallas import tpu as pltpu
from jax.sharding import PartitionSpec as P

f32 = jnp.float32
bf16 = jnp.bfloat16


def halves(value):
    high = value.astype(bf16)
    return high, (value - high.astype(f32)).astype(bf16)


ROWS = ((1,), (0,))
TURNED = ((1,), (1,))


def mul_halves(left, right, contract=ROWS):
    dims = (contract, ((), ()))
    a, b = left
    c, d = right
    rows = a.shape[0]
    both = lax.dot_general(jnp.concatenate([a, b], axis=0), c, dims, preferred_element_type=f32)
    return both[0:rows] + (both[rows:] + lax.dot_general(a, d, dims, preferred_element_type=f32))


def mul(left, right):
    return mul_halves(halves(left), halves(right))


def mul_nt(left, right):
    return mul_halves(halves(left), halves(right), TURNED)


def stack(*parts):
    return tuple(jnp.concatenate(group, axis=0) for group in zip(*parts))


def masks(size):
    rows = lax.broadcasted_iota(jnp.int32, (size, size), 0)
    cols = lax.broadcasted_iota(jnp.int32, (size, size), 1)
    return rows > cols, rows == cols


def rows8(vector):
    return jnp.broadcast_to(vector, (8, vector.shape[1]))


def invert(m, work):
    size = m.shape[0]
    _, diag = masks(size)
    eye = diag.astype(f32)
    magnitude = jnp.abs(m)
    bound = jnp.minimum(
        jnp.max(jnp.sum(magnitude, axis=1, keepdims=True)),
        jnp.max(jnp.sum(magnitude, axis=0, keepdims=True)),
    )
    scale = 2.0 / (2.0 + bound)
    work[0:size] = scale * eye
    work[size : 2 * size] = (1.0 - scale) * eye - scale * m

    def step(radius):
        square = radius * radius
        factor = 2.0 / (2.0 - square)
        whole = work[...]
        low = whole.astype(bf16)
        out = jnp.dot(low, low[size : 2 * size], preferred_element_type=f32)
        work[0:size] = factor * (whole[0:size] + out[0:size])
        work[size : 2 * size] = factor * out[size : 2 * size] + (1.0 - factor) * eye
        return square / (2.0 - square)

    lax.while_loop(
        lambda radius: radius > 1e-2, step, jnp.minimum(bound / (2.0 + bound), 1.0 - 1e-6)
    )
    split = halves(m)

    def more(carry):
        square_of, count = carry
        return jnp.logical_and(square_of > 2e-3, count < 60)

    def correct(carry):
        _, count = carry
        x = work[0:size]
        x_halves = halves(x)
        residual = eye - x - mul_halves(x_halves, split)
        low = residual.astype(bf16)
        square = jnp.dot(low, low, preferred_element_type=f32)
        square_of = jnp.max(jnp.sum(jnp.abs(square), axis=0, keepdims=True))
        bad = jnp.logical_and(count == 0, jnp.logical_not(square_of < 0.25))
        better = x + mul_halves(halves(residual + square), x_halves)
        work[0:size] = jnp.where(bad, scale * eye, better)
        return jnp.where(bad, 1.0, square_of), count + 1

    lax.while_loop(more, correct, (jnp.float32(1.0), jnp.int32(0)))
    return work[0:size]


def unpack(tail, linear, square):
    below, diag = masks(square.shape[0])
    turned = square.T
    upto = jnp.logical_or(below, diag)
    info = jnp.where(upto, square, turned)
    cov = jnp.where(upto, turned, square)
    cov = jnp.where(diag, tail[2:3], cov)
    return linear, tail[0:1], cov, tail[1:2], info


def unpack_whole(ref):
    size = ref.shape[1]
    return unpack(ref[0:8], ref[8 : size + 8], ref[size + 8 : 2 * size + 8])


def unpack_halves(got, far, core):
    size = got.shape[1]
    swap = core == 1
    own = got[...]
    other = far[...]
    head = jnp.where(swap, other, own)
    square = jnp.where(swap, own[8:], other[8:])
    return unpack(head[0:8], head[8:], square)


def dual(flag, element):
    linear, offset, cov, vector, info = element
    return (
        jnp.where(flag, linear.T, linear),
        jnp.where(flag, vector, offset),
        jnp.where(flag, info, cov),
        jnp.where(flag, -offset, vector),
        jnp.where(flag, cov, info),
    )


def ordered(flag, one, two):
    return (
        [jnp.where(flag, b, a) for a, b in zip(one, two)],
        [jnp.where(flag, a, b) for a, b in zip(one, two)],
    )


def pack(linear, offset, cov, vector, info):
    size = cov.shape[0]
    below, diag = masks(size)
    square = jnp.where(jnp.logical_or(below, diag), info, cov)
    diagonal = jnp.sum(jnp.where(diag, cov, 0.0), axis=0, keepdims=True)
    tail = jnp.concatenate([offset, vector, diagonal, jnp.zeros((5, size), f32)], axis=0)
    return jnp.concatenate([tail, linear, square], axis=0)


def fold(first, second, work):
    lin1, off1, cov1, vec1, inf1 = first
    lin2, off2, cov2, vec2, inf2 = second
    size = cov1.shape[0]
    cov1_halves = halves(cov1)
    lin1_halves = halves(lin1)
    lin2_halves = halves(lin2)
    inf2_halves = halves(inf2)
    top = mul_halves(stack(cov1_halves, halves(rows8(off1))), inf2_halves)
    pull = halves(rows8(vec2 - top[size : size + 1]))
    weight = halves(invert(top[0:size], work[0]))
    moved = halves(mul_halves(stack(lin2_halves, inf2_halves, pull), weight))
    lin_halves = tuple(part[0:size] for part in moved)
    left = mul_halves(moved, lin1_halves)
    spread = mul_halves(stack(lin_halves, halves(rows8(vec2))), cov1_halves)
    push = off1 + spread[size : size + 1]
    info = inf1 + mul(lin1.T, left[size : 2 * size])
    cov = cov2 + mul_halves(halves(spread[0:size]), lin2_halves, TURNED)
    offset = off2 + mul_halves(halves(rows8(push)), lin_halves, TURNED)[0:1]
    return left[0:size], offset, cov, vec1 + left[2 * size : 2 * size + 1], info


def half_fold(cov1, off1, second, work):
    lin2, off2, cov2, vec2, inf2 = second
    size = cov1.shape[0]
    cov1_halves = halves(cov1)
    lin2_halves = halves(lin2)
    weight = invert(mul_halves(cov1_halves, halves(inf2)), work[0])
    lin_halves = halves(mul_halves(lin2_halves, halves(weight)))
    spread = mul_halves(stack(lin_halves, halves(rows8(vec2))), cov1_halves)
    push = off1 + spread[size : size + 1]
    cov = cov2 + mul_halves(halves(spread[0:size]), lin2_halves, TURNED)
    offset = off2 + mul_halves(halves(rows8(push)), lin_halves, TURNED)[0:1]
    return cov, offset


def build_kernel(flags, trans, op_ref, rows, out, info_ref, work):
    slots, stations, width = op_ref.shape
    size = trans.shape[0]
    step = flags[0]
    value = rows[0:slots]
    noise = rows[slots : 2 * slots]

    def row(index):
        at = 2 * slots + 2 * index
        return jnp.concatenate([rows[at : at + 1], rows[at + 1 : at + 2]], axis=1)

    var_row, mean_row, start_row = row(0), row(1), row(2)
    count = rows[2 * slots + 6 : 2 * slots + 7, 0:1]
    blocks = rows[2 * slots + 7 : 2 * slots + 8]
    noise_cols = noise.T
    weighted = value / noise
    info_ref[...] = jnp.zeros(info_ref.shape, f32)
    shifts = []
    for a in range(size // width):
        info = jnp.zeros((width, width), f32)
        shift = jnp.zeros((8, width), f32)
        for m in range(slots):
            keep = jnp.logical_and(count > m, blocks[:, m : m + 1] == a).astype(f32)
            op = op_ref[m]
            wide = op.astype(f32)
            scaled = (wide / noise_cols[:, m : m + 1]).astype(bf16)
            part = lax.dot_general(
                scaled, op, (((0,), (0,)), ((), ())), preferred_element_type=f32
            )
            info = info + keep * part
            shift = shift + keep * jnp.dot(
                rows8(weighted[m : m + 1]),
                wide,
                precision=lax.Precision.HIGHEST,
                preferred_element_type=f32,
            )
        info = 0.5 * (info + info.T)
        info_ref[a * width : (a + 1) * width, a * width : (a + 1) * width] = info
        shifts.append(shift[0:1])
    h = jnp.concatenate(shifts, axis=1)
    info = info_ref[...]
    first = (step == 0).astype(f32)
    var = first * start_row + (1.0 - first) * var_row
    mean = first * mean_row
    moving = (1.0 - first) * trans[...]
    turned = invert(info * var, work)
    weight = turned.T
    cov = weight * var
    linear = mul(weight, moving)
    small = mul(rows8(h), jnp.concatenate([cov, linear], axis=1))
    offset = small[0:1, 0:size] + mul(rows8(mean), turned)[0:1]
    vector = small[0:1, size : 2 * size]
    info_moved = mul(moving.T, mul(info, linear))
    out[...] = pack(linear, offset, cov, vector, info_moved)


def put_sent(out, sent, core):
    size = out.shape[1]
    sent[...] = out[pl.ds(core * size, size + 8)]


def put_edge(cov, offset, sent):
    size = cov.shape[0]
    sent[0:8] = rows8(offset)
    sent[8 : size + 8] = cov


def pair_kernel(flags, mine, other, state, sent, sides, *work):
    size = mine.shape[1]
    core = flags[1]
    high = core == 1
    own = unpack_whole(mine)
    far = unpack_whole(other)
    whole = pack(*fold(*ordered(high, own, far), work))
    state[...] = whole
    put_sent(state, sent, core)
    _, diag = masks(size)
    eye = diag.astype(f32)
    none = jnp.zeros((8, size), f32)
    neutral = jnp.concatenate([none, eye, jnp.zeros((size, size), f32)], axis=0)
    sides[1] = jnp.where(high, whole, mine[...])
    sides[0] = jnp.where(high, neutral, pack(*dual(jnp.logical_not(high), far)))


def fold_kernel(flags, bits, state, got, far, out, sent, *work):
    core = flags[1]
    high = bits[0] == 1
    received = unpack_halves(got, far, core)
    out[...] = pack(*fold(*ordered(high, unpack_whole(out), received), work))
    put_sent(out, sent, core)


def edge_kernel(flags, bits, state, got, far, sent, *work):
    core = flags[1]
    high = bits[0] == 1
    upper = bits[1] == 1
    first, second = ordered(
        jnp.logical_xor(high, upper), unpack_whole(state), unpack_halves(got, far, core)
    )
    _, offset, cov, _, _ = dual(upper, first)
    cov, offset = half_fold(cov, offset, dual(upper, second), work)
    put_edge(cov, offset, sent)


def side_kernel(flags, bits, sides, got, far, out, *work):
    core = flags[1]
    bit = bits[0]
    received = dual(bit == 0, unpack_halves(got, far, core))
    out[bit] = pack(*fold(received, unpack_whole(out.at[bit]), work))


def two_sides_kernel(flags, bits, sides, got_a, far_a, got_b, far_b, out, received, *work):
    core = flags[1]

    def update(index, carry):
        bit = jnp.where(index == 0, bits[2], bits[0])

        @pl.when(index == 0)
        def _():
            received[...] = pack(*dual(bit == 0, unpack_halves(got_a, far_a, core)))

        @pl.when(index == 1)
        def _():
            received[...] = pack(*dual(bit == 0, unpack_halves(got_b, far_b, core)))

        out[bit] = pack(*fold(unpack_whole(received), unpack_whole(out.at[bit]), work))
        return carry

    lax.fori_loop(0, 2, update, 0)


def close_kernel(flags, bits, sides, got, far, out, one, two, three, *work):
    size = got.shape[1]
    core = flags[1]
    bit = bits[0]
    upper = bits[1] == 1
    _, diag = masks(size)
    one[...] = pack(*dual(bit == 0, unpack_halves(got, far, core)))
    two[...] = sides[bit]

    def turn(index, carry):
        three[...] = pack(*fold(unpack_whole(one), unpack_whole(two), work))

        @pl.when(index == 0)
        def _():
            fresh = unpack_whole(three)
            kept = unpack_whole(sides.at[1 - bit])
            back, front = ordered(bit == 1, fresh, kept)
            eye = diag.astype(f32)
            back_lin, back_off, back_cov, back_vec, back_inf = back
            front_lin, mean, cov, front_vec, front_inf = front
            none = jnp.zeros((1, size), f32)
            zero = jnp.zeros((size, size), f32)
            one[...] = pack(
                jnp.where(upper, front_lin, cov),
                mean,
                cov,
                jnp.where(upper, front_vec, none),
                jnp.where(upper, front_inf, zero),
            )
            two[...] = pack(
                jnp.where(upper, eye, back_lin.T),
                jnp.where(upper, none, -back_vec),
                jnp.where(upper, zero, back_inf),
                back_off,
                back_cov,
            )

        return carry

    lax.fori_loop(0, 2, turn, 0)
    linear, offset, spread, vector, info = unpack_whole(three)
    _, mean, cov, _, _ = unpack_whole(one)
    base = jnp.where(upper, spread, cov - info)
    base = jnp.sum(jnp.where(diag, base, 0.0), axis=0, keepdims=True)
    out[0:8] = jnp.concatenate(
        [
            jnp.where(upper, vector, -offset),
            jnp.where(upper, offset, mean + vector),
            base,
            jnp.zeros((5, size), f32),
        ],
        axis=0,
    )
    out[8 : size + 8] = jnp.where(upper, linear.T, linear)
    out[size + 8 : 2 * size + 8] = jnp.where(upper, info, spread)


def last_kernel(flags, bits, closed, received, mean_out, var_out, work):
    size = received.shape[1]
    sign = (2 * bits[1] - 1).astype(f32)
    matrix = received[8 : size + 8]
    rows = closed[0:8]
    turned = closed[8 : size + 8]
    spread = mul(matrix, turned)
    push = received[0:1] + mul(rows8(rows[0:1]), matrix)[0:1]
    weight = invert(mul(matrix, closed[size + 8 : 2 * size + 8]), work)
    moved = mul_nt(rows8(push), weight)
    mean_out[...] = rows[1:2] + mul(moved, turned)[0:1]
    var_out[...] = rows[2:3] + sign * jnp.sum(
        turned * mul(weight, spread), axis=0, keepdims=True
    )


def run(body, out_shapes, size, *args, scalars=0, extra=(), aliases={}):
    vmem = pl.BlockSpec(memory_space=pltpu.VMEM)
    spaces = [
        pl.BlockSpec(memory_space=pltpu.SMEM) if index < scalars else vmem
        for index in range(len(args))
    ]
    single = len(out_shapes) == 1
    shapes = [jax.ShapeDtypeStruct(shape, f32) for shape in out_shapes]
    return pl.pallas_call(
        body,
        out_shape=shapes[0] if single else shapes,
        in_specs=spaces,
        out_specs=vmem if single else [vmem] * len(shapes),
        scratch_shapes=list(extra),
        input_output_aliases=aliases,
        compiler_params=pltpu.CompilerParams(vmem_limit_bytes=16 * 1024 * 1024),
        name=body.__name__,
    )(*args)


def local(
    transition, noise_var, prior_mean, prior_var, obs_op, obs_value, obs_noise, obs_block, obs_count
):
    size = transition.shape[0]
    devices = lax.axis_size("tm")
    levels = (devices - 1).bit_length()
    device = lax.axis_index("tm")
    core = device % 2
    flags = jnp.stack([device, core]).astype(jnp.int32)
    _, slots, stations, width = obs_op.shape
    assert size == 2 * stations
    tall = 2 * slots + 8

    def placed(value, at):
        value = value.astype(f32)
        return jnp.pad(value, ((at, tall - at - value.shape[0]), (0, stations - value.shape[1])))

    rows = (
        placed(obs_value[0], 0)
        + placed(obs_noise[0], slots)
        + placed(noise_var.reshape(2, stations), 2 * slots)
        + placed(prior_mean.reshape(2, stations), 2 * slots + 2)
        + placed(prior_var.reshape(2, stations), 2 * slots + 4)
        + placed(obs_count[:, None], 2 * slots + 6)
        + placed(obs_block, 2 * slots + 7)
    )
    message = (2 * size + 8, size)
    half = (size + 8, size)
    inverse_work = [pltpu.VMEM((2 * size, size), f32)]

    def traded(value, level):
        return lax.ppermute(value, "tm", [(d, d ^ (1 << level)) for d in range(devices)])

    element = run(
        build_kernel,
        [message],
        size,
        flags,
        transition,
        obs_op[0],
        rows,
        scalars=1,
        extra=[pltpu.VMEM((size, size), f32)] + inverse_work,
    )
    other = traded(element, 0)
    state, sent, sides = run(
        pair_kernel,
        [message, half, (2,) + message],
        size,
        flags,
        element,
        other,
        scalars=1,
        extra=inverse_work,
    )
    for level in range(1, levels - 1):
        bits = jnp.stack([(device >> (level + k)) % 2 for k in (0, 1, -1)]).astype(jnp.int32)
        got = traded(sent, level)
        got, sides = lax.optimization_barrier((got, sides))
        far = traded(got, 0)
        now = (flags, bits, state, got, far)
        if level < levels - 2:
            state, sent = run(
                fold_kernel,
                [message, half],
                size,
                *now,
                scalars=2,
                extra=inverse_work,
                aliases={2: 0},
            )
        else:
            sent = run(edge_kernel, [half], size, *now, scalars=2, extra=inverse_work)
        _, sides = lax.optimization_barrier((sent, sides))
        now = (flags, bits, sides, got, far)
        if level < levels - 2 and (level > 1 and level % 2 == 0):
            waiting = (got, far)
        elif level < levels - 2 and level > 1:
            sides = run(
                two_sides_kernel,
                [(2,) + message],
                size,
                flags,
                bits,
                sides,
                *waiting,
                got,
                far,
                scalars=2,
                extra=[pltpu.VMEM(message, f32)] + inverse_work,
                aliases={2: 0},
            )
        elif level == 1:
            sides = run(
                side_kernel,
                [(2,) + message],
                size,
                *now,
                scalars=2,
                extra=inverse_work,
                aliases={2: 0},
            )
        else:
            closed = run(
                close_kernel,
                [message],
                size,
                *now,
                scalars=2,
                extra=[pltpu.VMEM(message, f32)] * 3 + inverse_work,
            )
    received = traded(sent, levels - 1)
    mean, var = run(
        last_kernel,
        [(1, size), (1, size)],
        size,
        flags,
        bits,
        closed,
        received,
        scalars=2,
        extra=inverse_work,
    )
    return mean, var


def solution(mesh):
    return jax.shard_map(
        local,
        mesh=mesh,
        in_specs=(
            P(),
            P(),
            P(),
            P(),
            P("tm", None, None, None),
            P("tm", None, None),
            P("tm", None, None),
            P("tm", None),
            P("tm"),
        ),
        out_specs=(P("tm", None), P("tm", None)),
        check_vma=False,
    )
```

```python
import functools

import jax
import jax.numpy as jnp
from jax import lax
from jax.experimental import pallas as pl
from jax.experimental.pallas import tpu as pltpu
from jax.sharding import PartitionSpec as P

f32 = jnp.float32
bf16 = jnp.bfloat16


def halves(value):
    high = value.astype(bf16)
    return high, (value - high.astype(f32)).astype(bf16)


ROWS = ((1,), (0,))
TURNED = ((1,), (1,))


def mul_halves(left, right, contract=ROWS):
    dims = (contract, ((), ()))
    a, b = left
    c, d = right
    rows = a.shape[0]
    both = lax.dot_general(jnp.concatenate([a, b], axis=0), c, dims, preferred_element_type=f32)
    return both[0:rows] + (both[rows:] + lax.dot_general(a, d, dims, preferred_element_type=f32))


def mul(left, right):
    return mul_halves(halves(left), halves(right))


def mul_nt(left, right):
    return mul_halves(halves(left), halves(right), TURNED)


def stack(*parts):
    return tuple(jnp.concatenate(group, axis=0) for group in zip(*parts))


def masks(size):
    rows = lax.broadcasted_iota(jnp.int32, (size, size), 0)
    cols = lax.broadcasted_iota(jnp.int32, (size, size), 1)
    return rows > cols, rows == cols


def rows8(vector):
    return jnp.broadcast_to(vector, (8, vector.shape[1]))


def invert(m, work):
    size = m.shape[0]
    _, diag = masks(size)
    eye = diag.astype(f32)
    magnitude = jnp.abs(m)
    bound = jnp.minimum(
        jnp.max(jnp.sum(magnitude, axis=1, keepdims=True)),
        jnp.max(jnp.sum(magnitude, axis=0, keepdims=True)),
    )
    scale = 2.0 / (2.0 + bound)
    work[0:size] = scale * eye
    work[size : 2 * size] = (1.0 - scale) * eye - scale * m

    def step(radius):
        square = radius * radius
        factor = 2.0 / (2.0 - square)
        whole = work[...]
        lower = whole[size : 2 * size]
        ends = jnp.where(diag, lower, 0.0)
        across = jnp.sum(ends, axis=0, keepdims=True)
        down = jnp.sum(ends, axis=1, keepdims=True)
        low = whole.astype(bf16)
        rest = lower - ends
        rest_low = rest.astype(bf16)
        out = jnp.dot(
            jnp.concatenate([low[0:size], rest_low], axis=0), rest_low, preferred_element_type=f32
        )
        work[0:size] = factor * (whole[0:size] * (1.0 + across) + out[0:size])
        work[size : 2 * size] = factor * (
            out[size : 2 * size] + lower * across + rest * down
        ) + (1.0 - factor) * eye
        return square / (2.0 - square)

    lax.while_loop(
        lambda radius: radius > 2e-2, step, jnp.minimum(bound / (2.0 + bound), 1.0 - 1e-6)
    )
    split = halves(m)

    def more(carry):
        square_of, count = carry
        return jnp.logical_and(square_of > 2e-3, count < 60)

    def correct(carry):
        _, count = carry
        x = work[0:size]
        x_halves = halves(x)
        residual = eye - x - mul_halves(x_halves, split)
        low = residual.astype(bf16)
        square = jnp.dot(low, low, preferred_element_type=f32)
        square_of = jnp.max(jnp.sum(jnp.abs(square), axis=0, keepdims=True))
        bad = jnp.logical_and(count == 0, jnp.logical_not(square_of < 0.25))
        better = x + mul_halves(halves(residual + square), x_halves)
        work[0:size] = jnp.where(bad, scale * eye, better)
        return jnp.where(bad, 1.0, square_of), count + 1

    lax.while_loop(more, correct, (jnp.float32(1.0), jnp.int32(0)))
    return work[0:size]


def unpack(tail, linear, square):
    below, diag = masks(square.shape[0])
    turned = square.T
    upto = jnp.logical_or(below, diag)
    info = jnp.where(upto, square, turned)
    cov = jnp.where(upto, turned, square)
    cov = jnp.where(diag, tail[2:3], cov)
    return linear, tail[0:1], cov, tail[1:2], info


def unpack_whole(ref):
    size = ref.shape[1]
    return unpack(ref[0:8], ref[8 : size + 8], ref[size + 8 : 2 * size + 8])


def unpack_halves(got, far, core):
    size = got.shape[1]
    swap = core == 1
    own = got[...]
    other = far[...]
    head = jnp.where(swap, other, own)
    square = jnp.where(swap, own[8:], other[8:])
    return unpack(head[0:8], head[8:], square)


def dual(flag, element):
    linear, offset, cov, vector, info = element
    return (
        jnp.where(flag, linear.T, linear),
        jnp.where(flag, vector, offset),
        jnp.where(flag, info, cov),
        jnp.where(flag, -offset, vector),
        jnp.where(flag, cov, info),
    )


def ordered(flag, one, two):
    return (
        [jnp.where(flag, b, a) for a, b in zip(one, two)],
        [jnp.where(flag, a, b) for a, b in zip(one, two)],
    )


def pack(linear, offset, cov, vector, info):
    size = cov.shape[0]
    below, diag = masks(size)
    square = jnp.where(jnp.logical_or(below, diag), info, cov)
    diagonal = jnp.sum(jnp.where(diag, cov, 0.0), axis=0, keepdims=True)
    tail = jnp.concatenate([offset, vector, diagonal, jnp.zeros((5, size), f32)], axis=0)
    return jnp.concatenate([tail, linear, square], axis=0)


def fold(first, second, work):
    lin1, off1, cov1, vec1, inf1 = first
    lin2, off2, cov2, vec2, inf2 = second
    size = cov1.shape[0]
    cov1_halves = halves(cov1)
    lin1_halves = halves(lin1)
    lin2_halves = halves(lin2)
    inf2_halves = halves(inf2)
    top = mul_halves(stack(cov1_halves, halves(rows8(off1))), inf2_halves)
    pull = halves(rows8(vec2 - top[size : size + 1]))
    weight = halves(invert(top[0:size], work[0]))
    moved = halves(mul_halves(stack(lin2_halves, inf2_halves, pull), weight))
    lin_halves = tuple(part[0:size] for part in moved)
    left = mul_halves(moved, lin1_halves)
    spread = mul_halves(stack(lin_halves, halves(rows8(vec2))), cov1_halves)
    push = off1 + spread[size : size + 1]
    info = inf1 + mul(lin1.T, left[size : 2 * size])
    cov = cov2 + mul_halves(halves(spread[0:size]), lin2_halves, TURNED)
    offset = off2 + mul_halves(halves(rows8(push)), lin_halves, TURNED)[0:1]
    return left[0:size], offset, cov, vec1 + left[2 * size : 2 * size + 1], info


def half_fold(cov1, off1, second, work):
    lin2, off2, cov2, vec2, inf2 = second
    size = cov1.shape[0]
    cov1_halves = halves(cov1)
    lin2_halves = halves(lin2)
    weight = invert(mul_halves(cov1_halves, halves(inf2)), work[0])
    lin_halves = halves(mul_halves(lin2_halves, halves(weight)))
    spread = mul_halves(stack(lin_halves, halves(rows8(vec2))), cov1_halves)
    push = off1 + spread[size : size + 1]
    cov = cov2 + mul_halves(halves(spread[0:size]), lin2_halves, TURNED)
    offset = off2 + mul_halves(halves(rows8(push)), lin_halves, TURNED)[0:1]
    return cov, offset


def build_kernel(flags, trans, op_ref, rows, out, info_ref, work):
    slots, stations, width = op_ref.shape
    size = trans.shape[0]
    step = flags[0]
    value = rows[0:slots]
    noise = rows[slots : 2 * slots]

    def row(index):
        at = 2 * slots + 2 * index
        return jnp.concatenate([rows[at : at + 1], rows[at + 1 : at + 2]], axis=1)

    var_row, mean_row, start_row = row(0), row(1), row(2)
    count = rows[2 * slots + 6 : 2 * slots + 7, 0:1]
    blocks = rows[2 * slots + 7 : 2 * slots + 8]
    noise_cols = noise.T
    weighted = value / noise
    info_ref[...] = jnp.zeros(info_ref.shape, f32)
    infos = [jnp.zeros((width, width), f32) for _ in range(size // width)]
    shifts = [jnp.zeros((1, width), f32) for _ in range(size // width)]
    for m in range(slots):
        op = op_ref[m]
        scaled = (op.astype(f32) / noise_cols[:, m : m + 1]).astype(bf16)
        part = lax.dot_general(scaled, op, (((0,), (0,)), ((), ())), preferred_element_type=f32)
        both = jnp.concatenate(halves(rows8(weighted[m : m + 1])), axis=0)
        both = jnp.dot(both, op, preferred_element_type=f32)
        shift = both[0:1] + both[8:9]
        for a in range(size // width):
            keep = jnp.logical_and(count > m, blocks[:, m : m + 1] == a).astype(f32)
            infos[a] = infos[a] + keep * part
            shifts[a] = shifts[a] + keep * shift
    for a, info in enumerate(infos):
        info = 0.5 * (info + info.T)
        info_ref[a * width : (a + 1) * width, a * width : (a + 1) * width] = info
    h = jnp.concatenate(shifts, axis=1)
    info = info_ref[...]
    first = (step == 0).astype(f32)
    var = first * start_row + (1.0 - first) * var_row
    mean = first * mean_row
    moving = (1.0 - first) * trans[...]
    turned = invert(info * var, work)
    weight = turned.T
    cov = weight * var
    linear = mul(weight, moving)
    small = mul(rows8(h), jnp.concatenate([cov, linear], axis=1))
    offset = small[0:1, 0:size] + mul(rows8(mean), turned)[0:1]
    vector = small[0:1, size : 2 * size]
    info_moved = mul(moving.T, mul(info, linear))
    out[...] = pack(linear, offset, cov, vector, info_moved)


def put_sent(out, sent, core):
    size = out.shape[1]
    sent[...] = out[pl.ds(core * size, size + 8)]


def put_edge(cov, offset, sent):
    size = cov.shape[0]
    part = size // 2
    below, _ = masks(part)
    _, diag = masks(size)
    diagonal = jnp.sum(jnp.where(diag, cov, 0.0), axis=0, keepdims=True)
    sent[0:8] = jnp.concatenate([offset, diagonal, jnp.zeros((6, size), f32)], axis=0)
    shared = jnp.where(below, cov[0:part, 0:part], cov[part:, part:])
    sent[8 : part + 8] = jnp.concatenate([shared, cov[0:part, part:]], axis=1)


def take_edge(ref):
    size = ref.shape[1]
    part = size // 2
    below, _ = masks(part)
    _, diag = masks(size)
    shared = ref[8 : part + 8, 0:part]
    corner = ref[8 : part + 8, part:size]
    turned = shared.T
    cov = jnp.concatenate(
        [
            jnp.concatenate([jnp.where(below, shared, turned), corner], axis=1),
            jnp.concatenate([corner.T, jnp.where(below, turned, shared)], axis=1),
        ],
        axis=0,
    )
    return jnp.where(diag, ref[1:2], cov), ref[0:1]


def pair_kernel(flags, mine, other, state, sent, sides, *work):
    size = mine.shape[1]
    core = flags[1]
    high = core == 1
    own = unpack_whole(mine)
    far = unpack_whole(other)
    whole = pack(*fold(*ordered(high, own, far), work))
    state[...] = whole
    put_sent(state, sent, core)
    _, diag = masks(size)
    eye = diag.astype(f32)
    none = jnp.zeros((8, size), f32)
    neutral = jnp.concatenate([none, eye, jnp.zeros((size, size), f32)], axis=0)
    sides[1] = jnp.where(high, whole, mine[...])
    sides[0] = jnp.where(high, neutral, pack(*dual(jnp.logical_not(high), far)))


def fold_kernel(flags, bits, state, got, far, out, sent, *work):
    core = flags[1]
    high = bits[0] == 1
    received = unpack_halves(got, far, core)
    out[...] = pack(*fold(*ordered(high, unpack_whole(out), received), work))
    put_sent(out, sent, core)


def edge_kernel(flags, bits, state, got, far, sent, *work):
    core = flags[1]
    high = bits[0] == 1
    upper = bits[1] == 1
    first, second = ordered(
        jnp.logical_xor(high, upper), unpack_whole(state), unpack_halves(got, far, core)
    )
    _, offset, cov, _, _ = dual(upper, first)
    cov, offset = half_fold(cov, offset, dual(upper, second), work)
    put_edge(cov, offset, sent)


def side_kernel(flags, bits, sides, got, far, out, *work):
    core = flags[1]
    bit = bits[0]
    received = dual(bit == 0, unpack_halves(got, far, core))
    out[bit] = pack(*fold(received, unpack_whole(out.at[bit]), work))


def two_sides_kernel(flags, bits, sides, got_a, far_a, got_b, far_b, out, received, *work):
    core = flags[1]

    def update(index, carry):
        bit = jnp.where(index == 0, bits[2], bits[0])

        @pl.when(index == 0)
        def _():
            received[...] = pack(*dual(bit == 0, unpack_halves(got_a, far_a, core)))

        @pl.when(index == 1)
        def _():
            received[...] = pack(*dual(bit == 0, unpack_halves(got_b, far_b, core)))

        out[bit] = pack(*fold(unpack_whole(received), unpack_whole(out.at[bit]), work))
        return carry

    lax.fori_loop(0, 2, update, 0)


def close_kernel(flags, bits, sides, got, far, out, one, two, three, *work):
    size = got.shape[1]
    core = flags[1]
    bit = bits[0]
    upper = bits[1] == 1
    _, diag = masks(size)
    one[...] = pack(*dual(bit == 0, unpack_halves(got, far, core)))
    two[...] = sides[bit]

    def turn(index, carry):
        three[...] = pack(*fold(unpack_whole(one), unpack_whole(two), work))

        @pl.when(index == 0)
        def _():
            fresh = unpack_whole(three)
            kept = unpack_whole(sides.at[1 - bit])
            back, front = ordered(bit == 1, fresh, kept)
            eye = diag.astype(f32)
            back_lin, back_off, back_cov, back_vec, back_inf = back
            front_lin, mean, cov, front_vec, front_inf = front
            none = jnp.zeros((1, size), f32)
            zero = jnp.zeros((size, size), f32)
            one[...] = pack(
                jnp.where(upper, front_lin, cov),
                mean,
                cov,
                jnp.where(upper, front_vec, none),
                jnp.where(upper, front_inf, zero),
            )
            two[...] = pack(
                jnp.where(upper, eye, back_lin.T),
                jnp.where(upper, none, -back_vec),
                jnp.where(upper, zero, back_inf),
                back_off,
                back_cov,
            )

        return carry

    lax.fori_loop(0, 2, turn, 0)
    linear, offset, spread, vector, info = unpack_whole(three)
    _, mean, cov, _, _ = unpack_whole(one)
    base = jnp.where(upper, spread, cov - info)
    base = jnp.sum(jnp.where(diag, base, 0.0), axis=0, keepdims=True)
    out[0:8] = jnp.concatenate(
        [
            jnp.where(upper, vector, -offset),
            jnp.where(upper, offset, mean + vector),
            base,
            jnp.zeros((5, size), f32),
        ],
        axis=0,
    )
    out[8 : size + 8] = jnp.where(upper, linear.T, linear)
    out[size + 8 : 2 * size + 8] = jnp.where(upper, info, spread)


def last_kernel(flags, bits, closed, received, mean_out, var_out, work):
    size = received.shape[1]
    sign = (2 * bits[1] - 1).astype(f32)
    matrix, offset = take_edge(received)
    rows = closed[0:8]
    turned = closed[8 : size + 8]
    spread = mul(matrix, turned)
    push = offset + mul(rows8(rows[0:1]), matrix)[0:1]
    weight = invert(mul(matrix, closed[size + 8 : 2 * size + 8]), work)
    moved = mul_nt(rows8(push), weight)
    mean_out[...] = rows[1:2] + mul(moved, turned)[0:1]
    var_out[...] = rows[2:3] + sign * jnp.sum(
        turned * mul(weight, spread), axis=0, keepdims=True
    )


def run(body, out_shapes, size, *args, scalars=0, extra=(), aliases={}):
    vmem = pl.BlockSpec(memory_space=pltpu.VMEM)
    spaces = [
        pl.BlockSpec(memory_space=pltpu.SMEM) if index < scalars else vmem
        for index in range(len(args))
    ]
    single = len(out_shapes) == 1
    shapes = [jax.ShapeDtypeStruct(shape, f32) for shape in out_shapes]
    return pl.pallas_call(
        body,
        out_shape=shapes[0] if single else shapes,
        in_specs=spaces,
        out_specs=vmem if single else [vmem] * len(shapes),
        scratch_shapes=list(extra),
        input_output_aliases=aliases,
        compiler_params=pltpu.CompilerParams(vmem_limit_bytes=16 * 1024 * 1024),
        name=body.__name__,
    )(*args)


def local(
    transition, noise_var, prior_mean, prior_var, obs_op, obs_value, obs_noise, obs_block, obs_count
):
    size = transition.shape[0]
    devices = lax.axis_size("tm")
    levels = (devices - 1).bit_length()
    device = lax.axis_index("tm")
    core = device % 2
    flags = jnp.stack([device, core]).astype(jnp.int32)
    _, slots, stations, width = obs_op.shape
    assert size == 2 * stations
    tall = 2 * slots + 8

    def placed(value, at):
        value = value.astype(f32)
        return jnp.pad(value, ((at, tall - at - value.shape[0]), (0, stations - value.shape[1])))

    rows = (
        placed(obs_value[0], 0)
        + placed(obs_noise[0], slots)
        + placed(noise_var.reshape(2, stations), 2 * slots)
        + placed(prior_mean.reshape(2, stations), 2 * slots + 2)
        + placed(prior_var.reshape(2, stations), 2 * slots + 4)
        + placed(obs_count[:, None], 2 * slots + 6)
        + placed(obs_block, 2 * slots + 7)
    )
    message = (2 * size + 8, size)
    half = (size + 8, size)
    inverse_work = [pltpu.VMEM((2 * size, size), f32)]

    def traded(value, level):
        return lax.ppermute(value, "tm", [(d, d ^ (1 << level)) for d in range(devices)])

    element = run(
        build_kernel,
        [message],
        size,
        flags,
        transition,
        obs_op[0],
        rows,
        scalars=1,
        extra=[pltpu.VMEM((size, size), f32)] + inverse_work,
    )
    other = traded(element, 0)
    state, sent, sides = run(
        pair_kernel,
        [message, half, (2,) + message],
        size,
        flags,
        element,
        other,
        scalars=1,
        extra=inverse_work,
    )
    for level in range(1, levels - 1):
        bits = jnp.stack([(device >> (level + k)) % 2 for k in (0, 1, -1)]).astype(jnp.int32)
        got = traded(sent, level)
        got, sides = lax.optimization_barrier((got, sides))
        far = traded(got, 0)
        now = (flags, bits, state, got, far)
        if level < levels - 2:
            state, sent = run(
                fold_kernel,
                [message, half],
                size,
                *now,
                scalars=2,
                extra=inverse_work,
                aliases={2: 0},
            )
        else:
            sent = run(edge_kernel, [(size // 2 + 8, size)], size, *now, scalars=2, extra=inverse_work)
        _, sides = lax.optimization_barrier((sent, sides))
        now = (flags, bits, sides, got, far)
        if level < levels - 2 and (level > 1 and level % 2 == 0):
            waiting = (got, far)
        elif level < levels - 2 and level > 1:
            sides = run(
                two_sides_kernel,
                [(2,) + message],
                size,
                flags,
                bits,
                sides,
                *waiting,
                got,
                far,
                scalars=2,
                extra=[pltpu.VMEM(message, f32)] + inverse_work,
                aliases={2: 0},
            )
        elif level == 1:
            sides = run(
                side_kernel,
                [(2,) + message],
                size,
                *now,
                scalars=2,
                extra=inverse_work,
                aliases={2: 0},
            )
        else:
            closed = run(
                close_kernel,
                [message],
                size,
                *now,
                scalars=2,
                extra=[pltpu.VMEM(message, f32)] * 3 + inverse_work,
            )
    received = traded(sent, levels - 1)
    mean, var = run(
        last_kernel,
        [(1, size), (1, size)],
        size,
        flags,
        bits,
        closed,
        received,
        scalars=2,
        extra=inverse_work,
    )
    return mean, var


def solution(mesh):
    return jax.shard_map(
        local,
        mesh=mesh,
        in_specs=(
            P(),
            P(),
            P(),
            P(),
            P("tm", None, None, None),
            P("tm", None, None),
            P("tm", None, None),
            P("tm", None),
            P("tm"),
        ),
        out_specs=(P("tm", None), P("tm", None)),
        check_vma=False,
    )
```

```python
import functools

import jax
import jax.numpy as jnp
from jax import lax
from jax.experimental import pallas as pl
from jax.experimental.pallas import tpu as pltpu
from jax.sharding import PartitionSpec as P

f32 = jnp.float32
bf16 = jnp.bfloat16


def halves(value):
    high = value.astype(bf16)
    return high, (value - high.astype(f32)).astype(bf16)


ROWS = ((1,), (0,))
TURNED = ((1,), (1,))


def mul_halves(left, right, contract=ROWS):
    dims = (contract, ((), ()))
    a, b = left
    c, d = right
    rows = a.shape[0]
    both = lax.dot_general(jnp.concatenate([a, b], axis=0), c, dims, preferred_element_type=f32)
    return both[0:rows] + (both[rows:] + lax.dot_general(a, d, dims, preferred_element_type=f32))


def mul(left, right):
    return mul_halves(halves(left), halves(right))


def mul_nt(left, right):
    return mul_halves(halves(left), halves(right), TURNED)


def stack(*parts):
    return tuple(jnp.concatenate(group, axis=0) for group in zip(*parts))


def masks(size):
    rows = lax.broadcasted_iota(jnp.int32, (size, size), 0)
    cols = lax.broadcasted_iota(jnp.int32, (size, size), 1)
    return rows > cols, rows == cols


def rows8(vector):
    return jnp.broadcast_to(vector, (8, vector.shape[1]))


def invert(m, work):
    size = m.shape[0]
    _, diag = masks(size)
    eye = diag.astype(f32)
    magnitude = jnp.abs(m)
    bound = jnp.max(jnp.sum(magnitude, axis=0, keepdims=True))
    scale = 2.0 / (2.0 + bound)
    work[0:size] = scale * eye
    work[size : 2 * size] = (1.0 - scale) * eye - scale * m

    def step(radius):
        square = radius * radius
        factor = 2.0 / (2.0 - square)
        whole = work[...]
        lower = whole[size : 2 * size]
        ends = jnp.where(diag, lower, 0.0)
        across = jnp.sum(ends, axis=0, keepdims=True)
        down = jnp.sum(ends, axis=1, keepdims=True)
        low = whole.astype(bf16)
        rest = lower - ends
        rest_low = rest.astype(bf16)
        out = jnp.dot(
            jnp.concatenate([low[0:size], rest_low], axis=0), rest_low, preferred_element_type=f32
        )
        work[0:size] = factor * (whole[0:size] * (1.0 + across) + out[0:size])
        work[size : 2 * size] = factor * (
            out[size : 2 * size] + lower * across + rest * down
        ) + (1.0 - factor) * eye
        return square / (2.0 - square)

    lax.while_loop(
        lambda radius: radius > 2e-2, step, jnp.minimum(bound / (2.0 + bound), 1.0 - 1e-6)
    )
    split = halves(m)

    def more(carry):
        square_of, count = carry
        return jnp.logical_and(square_of > 2e-3, count < 60)

    def correct(carry):
        _, count = carry
        x = work[0:size]
        x_halves = halves(x)
        residual = eye - x - mul_halves(x_halves, split)
        low = residual.astype(bf16)
        square = jnp.dot(low, low, preferred_element_type=f32)
        square_of = jnp.max(jnp.sum(jnp.abs(square), axis=0, keepdims=True))
        bad = jnp.logical_and(count == 0, jnp.logical_not(square_of < 0.25))
        better = x + mul_halves(halves(residual + square), x_halves)
        work[0:size] = jnp.where(bad, scale * eye, better)
        return jnp.where(bad, 1.0, square_of), count + 1

    lax.while_loop(more, correct, (jnp.float32(1.0), jnp.int32(0)))
    return work[0:size]


def unpack(tail, linear, square):
    below, diag = masks(square.shape[0])
    turned = square.T
    upto = jnp.logical_or(below, diag)
    info = jnp.where(upto, square, turned)
    cov = jnp.where(upto, turned, square)
    cov = jnp.where(diag, tail[2:3], cov)
    return linear, tail[0:1], cov, tail[1:2], info


def unpack_whole(ref):
    size = ref.shape[1]
    return unpack(ref[0:8], ref[8 : size + 8], ref[size + 8 : 2 * size + 8])


def unpack_halves(got, far, core):
    size = got.shape[1]
    swap = core == 1
    own = got[...]
    other = far[...]
    head = jnp.where(swap, other, own)
    square = jnp.where(swap, own[8:], other[8:])
    return unpack(head[0:8], head[8:], square)


def dual(flag, element):
    linear, offset, cov, vector, info = element
    return (
        jnp.where(flag, linear.T, linear),
        jnp.where(flag, vector, offset),
        jnp.where(flag, info, cov),
        jnp.where(flag, -offset, vector),
        jnp.where(flag, cov, info),
    )


def ordered(flag, one, two):
    return (
        [jnp.where(flag, b, a) for a, b in zip(one, two)],
        [jnp.where(flag, a, b) for a, b in zip(one, two)],
    )


def pack(linear, offset, cov, vector, info):
    size = cov.shape[0]
    below, diag = masks(size)
    square = jnp.where(jnp.logical_or(below, diag), info, cov)
    diagonal = jnp.sum(jnp.where(diag, cov, 0.0), axis=0, keepdims=True)
    tail = jnp.concatenate([offset, vector, diagonal, jnp.zeros((5, size), f32)], axis=0)
    return jnp.concatenate([tail, linear, square], axis=0)


def fold(first, second, work):
    lin1, off1, cov1, vec1, inf1 = first
    lin2, off2, cov2, vec2, inf2 = second
    size = cov1.shape[0]
    cov1_halves = halves(cov1)
    lin1_halves = halves(lin1)
    lin2_halves = halves(lin2)
    inf2_halves = halves(inf2)
    top = mul_halves(stack(cov1_halves, halves(rows8(off1))), inf2_halves)
    pull = halves(rows8(vec2 - top[size : size + 1]))
    weight = halves(invert(top[0:size], work[0]))
    moved = halves(mul_halves(stack(lin2_halves, inf2_halves, pull), weight))
    lin_halves = tuple(part[0:size] for part in moved)
    left = mul_halves(moved, lin1_halves)
    spread = mul_halves(stack(lin_halves, halves(rows8(vec2))), cov1_halves)
    push = off1 + spread[size : size + 1]
    info = inf1 + mul(lin1.T, left[size : 2 * size])
    cov = cov2 + mul_halves(halves(spread[0:size]), lin2_halves, TURNED)
    offset = off2 + mul_halves(halves(rows8(push)), lin_halves, TURNED)[0:1]
    return left[0:size], offset, cov, vec1 + left[2 * size : 2 * size + 1], info


def half_fold(cov1, off1, second, work):
    lin2, off2, cov2, vec2, inf2 = second
    size = cov1.shape[0]
    cov1_halves = halves(cov1)
    lin2_halves = halves(lin2)
    weight = invert(mul_halves(cov1_halves, halves(inf2)), work[0])
    lin_halves = halves(mul_halves(lin2_halves, halves(weight)))
    spread = mul_halves(stack(lin_halves, halves(rows8(vec2))), cov1_halves)
    push = off1 + spread[size : size + 1]
    cov = cov2 + mul_halves(halves(spread[0:size]), lin2_halves, TURNED)
    offset = off2 + mul_halves(halves(rows8(push)), lin_halves, TURNED)[0:1]
    return cov, offset


def build_kernel(flags, trans, op_ref, rows, out, info_ref, work):
    slots, stations, width = op_ref.shape
    size = trans.shape[0]
    step = flags[0]
    value = rows[0:slots]
    noise = rows[slots : 2 * slots]

    def row(index):
        at = 2 * slots + 2 * index
        return jnp.concatenate([rows[at : at + 1], rows[at + 1 : at + 2]], axis=1)

    var_row, mean_row, start_row = row(0), row(1), row(2)
    count = rows[2 * slots + 6 : 2 * slots + 7, 0:1]
    blocks = rows[2 * slots + 7 : 2 * slots + 8]
    noise_cols = noise.T
    weighted = value / noise
    info_ref[...] = jnp.zeros(info_ref.shape, f32)
    infos = [jnp.zeros((width, width), f32) for _ in range(size // width)]
    shifts = [jnp.zeros((1, width), f32) for _ in range(size // width)]
    for m in range(slots):
        op = op_ref[m]
        scaled = (op.astype(f32) / noise_cols[:, m : m + 1]).astype(bf16)
        part = lax.dot_general(scaled, op, (((0,), (0,)), ((), ())), preferred_element_type=f32)
        both = jnp.concatenate(halves(rows8(weighted[m : m + 1])), axis=0)
        both = jnp.dot(both, op, preferred_element_type=f32)
        shift = both[0:1] + both[8:9]
        for a in range(size // width):
            keep = jnp.logical_and(count > m, blocks[:, m : m + 1] == a).astype(f32)
            infos[a] = infos[a] + keep * part
            shifts[a] = shifts[a] + keep * shift
    for a, info in enumerate(infos):
        info = 0.5 * (info + info.T)
        info_ref[a * width : (a + 1) * width, a * width : (a + 1) * width] = info
    h = jnp.concatenate(shifts, axis=1)
    info = info_ref[...]
    first = (step == 0).astype(f32)
    var = first * start_row + (1.0 - first) * var_row
    mean = first * mean_row
    moving = (1.0 - first) * trans[...]
    turned = invert(info * var, work)
    weight = turned.T
    cov = weight * var
    linear = mul(weight, moving)
    small = mul(rows8(h), jnp.concatenate([cov, linear], axis=1))
    offset = small[0:1, 0:size] + mul(rows8(mean), turned)[0:1]
    vector = small[0:1, size : 2 * size]
    info_moved = mul(moving.T, mul(info, linear))
    out[...] = pack(linear, offset, cov, vector, info_moved)


def put_sent(out, sent, core):
    size = out.shape[1]
    sent[...] = out[pl.ds(core * size, size + 8)]


def put_edge(cov, offset, sent):
    size = cov.shape[0]
    part = size // 2
    below, _ = masks(part)
    _, diag = masks(size)
    diagonal = jnp.sum(jnp.where(diag, cov, 0.0), axis=0, keepdims=True)
    sent[0:8] = jnp.concatenate([offset, diagonal, jnp.zeros((6, size), f32)], axis=0)
    shared = jnp.where(below, cov[0:part, 0:part], cov[part:, part:])
    sent[8 : part + 8] = jnp.concatenate([shared, cov[0:part, part:]], axis=1)


def take_edge(ref):
    size = ref.shape[1]
    part = size // 2
    below, _ = masks(part)
    _, diag = masks(size)
    shared = ref[8 : part + 8, 0:part]
    corner = ref[8 : part + 8, part:size]
    turned = shared.T
    cov = jnp.concatenate(
        [
            jnp.concatenate([jnp.where(below, shared, turned), corner], axis=1),
            jnp.concatenate([corner.T, jnp.where(below, turned, shared)], axis=1),
        ],
        axis=0,
    )
    return jnp.where(diag, ref[1:2], cov), ref[0:1]


def pair_kernel(flags, mine, other, state, sent, sides, *work):
    size = mine.shape[1]
    core = flags[1]
    high = core == 1
    own = unpack_whole(mine)
    far = unpack_whole(other)
    whole = pack(*fold(*ordered(high, own, far), work))
    state[...] = whole
    put_sent(state, sent, core)
    _, diag = masks(size)
    eye = diag.astype(f32)
    none = jnp.zeros((8, size), f32)
    neutral = jnp.concatenate([none, eye, jnp.zeros((size, size), f32)], axis=0)
    sides[1] = jnp.where(high, whole, mine[...])
    sides[0] = jnp.where(high, neutral, pack(*dual(jnp.logical_not(high), far)))


def fold_kernel(flags, bits, state, got, far, out, sent, *work):
    core = flags[1]
    high = bits[0] == 1
    received = unpack_halves(got, far, core)
    out[...] = pack(*fold(*ordered(high, unpack_whole(out), received), work))
    put_sent(out, sent, core)


def edge_kernel(flags, bits, state, got, far, sent, *work):
    core = flags[1]
    high = bits[0] == 1
    upper = bits[1] == 1
    first, second = ordered(
        jnp.logical_xor(high, upper), unpack_whole(state), unpack_halves(got, far, core)
    )
    _, offset, cov, _, _ = dual(upper, first)
    cov, offset = half_fold(cov, offset, dual(upper, second), work)
    put_edge(cov, offset, sent)


def side_kernel(flags, bits, sides, got, far, out, *work):
    core = flags[1]
    bit = bits[0]
    received = dual(bit == 0, unpack_halves(got, far, core))
    out[bit] = pack(*fold(received, unpack_whole(out.at[bit]), work))


def two_sides_kernel(flags, bits, sides, got_a, far_a, got_b, far_b, out, received, *work):
    core = flags[1]

    def update(index, carry):
        bit = jnp.where(index == 0, bits[2], bits[0])

        @pl.when(index == 0)
        def _():
            received[...] = pack(*dual(bit == 0, unpack_halves(got_a, far_a, core)))

        @pl.when(index == 1)
        def _():
            received[...] = pack(*dual(bit == 0, unpack_halves(got_b, far_b, core)))

        out[bit] = pack(*fold(unpack_whole(received), unpack_whole(out.at[bit]), work))
        return carry

    lax.fori_loop(0, 2, update, 0)


def close_kernel(flags, bits, sides, got, far, out, one, two, three, *work):
    size = got.shape[1]
    core = flags[1]
    bit = bits[0]
    upper = bits[1] == 1
    _, diag = masks(size)
    one[...] = pack(*dual(bit == 0, unpack_halves(got, far, core)))
    two[...] = sides[bit]

    def turn(index, carry):
        three[...] = pack(*fold(unpack_whole(one), unpack_whole(two), work))

        @pl.when(index == 0)
        def _():
            fresh = unpack_whole(three)
            kept = unpack_whole(sides.at[1 - bit])
            back, front = ordered(bit == 1, fresh, kept)
            eye = diag.astype(f32)
            back_lin, back_off, back_cov, back_vec, back_inf = back
            front_lin, mean, cov, front_vec, front_inf = front
            none = jnp.zeros((1, size), f32)
            zero = jnp.zeros((size, size), f32)
            one[...] = pack(
                jnp.where(upper, front_lin, cov),
                mean,
                cov,
                jnp.where(upper, front_vec, none),
                jnp.where(upper, front_inf, zero),
            )
            two[...] = pack(
                jnp.where(upper, eye, back_lin.T),
                jnp.where(upper, none, -back_vec),
                jnp.where(upper, zero, back_inf),
                back_off,
                back_cov,
            )

        return carry

    lax.fori_loop(0, 2, turn, 0)
    linear, offset, spread, vector, info = unpack_whole(three)
    _, mean, cov, _, _ = unpack_whole(one)
    base = jnp.where(upper, spread, cov - info)
    base = jnp.sum(jnp.where(diag, base, 0.0), axis=0, keepdims=True)
    out[0:8] = jnp.concatenate(
        [
            jnp.where(upper, vector, -offset),
            jnp.where(upper, offset, mean + vector),
            base,
            jnp.zeros((5, size), f32),
        ],
        axis=0,
    )
    out[8 : size + 8] = jnp.where(upper, linear.T, linear)
    out[size + 8 : 2 * size + 8] = jnp.where(upper, info, spread)


def last_kernel(flags, bits, closed, received, mean_out, var_out, work):
    size = received.shape[1]
    sign = (2 * bits[1] - 1).astype(f32)
    matrix, offset = take_edge(received)
    rows = closed[0:8]
    turned = closed[8 : size + 8]
    spread = mul(matrix, turned)
    push = offset + mul(rows8(rows[0:1]), matrix)[0:1]
    weight = invert(mul(matrix, closed[size + 8 : 2 * size + 8]), work)
    moved = mul_nt(rows8(push), weight)
    mean_out[...] = rows[1:2] + mul(moved, turned)[0:1]
    var_out[...] = rows[2:3] + sign * jnp.sum(
        turned * mul(weight, spread), axis=0, keepdims=True
    )


def run(body, out_shapes, size, *args, scalars=0, extra=(), aliases={}):
    vmem = pl.BlockSpec(memory_space=pltpu.VMEM)
    spaces = [
        pl.BlockSpec(memory_space=pltpu.SMEM) if index < scalars else vmem
        for index in range(len(args))
    ]
    single = len(out_shapes) == 1
    shapes = [jax.ShapeDtypeStruct(shape, f32) for shape in out_shapes]
    return pl.pallas_call(
        body,
        out_shape=shapes[0] if single else shapes,
        in_specs=spaces,
        out_specs=vmem if single else [vmem] * len(shapes),
        scratch_shapes=list(extra),
        input_output_aliases=aliases,
        compiler_params=pltpu.CompilerParams(vmem_limit_bytes=16 * 1024 * 1024),
        name=body.__name__,
    )(*args)


def local(
    transition, noise_var, prior_mean, prior_var, obs_op, obs_value, obs_noise, obs_block, obs_count
):
    size = transition.shape[0]
    devices = lax.axis_size("tm")
    levels = (devices - 1).bit_length()
    device = lax.axis_index("tm")
    core = device % 2
    flags = jnp.stack([device, core]).astype(jnp.int32)
    _, slots, stations, width = obs_op.shape
    assert size == 2 * stations
    tall = 2 * slots + 8

    def placed(value, at):
        value = value.astype(f32)
        return jnp.pad(value, ((at, tall - at - value.shape[0]), (0, stations - value.shape[1])))

    rows = (
        placed(obs_value[0], 0)
        + placed(obs_noise[0], slots)
        + placed(noise_var.reshape(2, stations), 2 * slots)
        + placed(prior_mean.reshape(2, stations), 2 * slots + 2)
        + placed(prior_var.reshape(2, stations), 2 * slots + 4)
        + placed(obs_count[:, None], 2 * slots + 6)
        + placed(obs_block, 2 * slots + 7)
    )
    message = (2 * size + 8, size)
    half = (size + 8, size)
    inverse_work = [pltpu.VMEM((2 * size, size), f32)]

    def traded(value, level):
        return lax.ppermute(value, "tm", [(d, d ^ (1 << level)) for d in range(devices)])

    element = run(
        build_kernel,
        [message],
        size,
        flags,
        transition,
        obs_op[0],
        rows,
        scalars=1,
        extra=[pltpu.VMEM((size, size), f32)] + inverse_work,
    )
    other = traded(element, 0)
    state, sent, sides = run(
        pair_kernel,
        [message, half, (2,) + message],
        size,
        flags,
        element,
        other,
        scalars=1,
        extra=inverse_work,
    )
    for level in range(1, levels - 1):
        bits = jnp.stack([(device >> (level + k)) % 2 for k in (0, 1, -1)]).astype(jnp.int32)
        got = traded(sent, level)
        got, sides = lax.optimization_barrier((got, sides))
        far = traded(got, 0)
        now = (flags, bits, state, got, far)
        if level < levels - 2:
            state, sent = run(
                fold_kernel,
                [message, half],
                size,
                *now,
                scalars=2,
                extra=inverse_work,
                aliases={2: 0},
            )
        else:
            sent = run(edge_kernel, [(size // 2 + 8, size)], size, *now, scalars=2, extra=inverse_work)
        _, sides = lax.optimization_barrier((sent, sides))
        now = (flags, bits, sides, got, far)
        if level < levels - 2 and (level > 1 and level % 2 == 0):
            waiting = (got, far)
        elif level < levels - 2 and level > 1:
            sides = run(
                two_sides_kernel,
                [(2,) + message],
                size,
                flags,
                bits,
                sides,
                *waiting,
                got,
                far,
                scalars=2,
                extra=[pltpu.VMEM(message, f32)] + inverse_work,
                aliases={2: 0},
            )
        elif level == 1:
            sides = run(
                side_kernel,
                [(2,) + message],
                size,
                *now,
                scalars=2,
                extra=inverse_work,
                aliases={2: 0},
            )
        else:
            closed = run(
                close_kernel,
                [message],
                size,
                *now,
                scalars=2,
                extra=[pltpu.VMEM(message, f32)] * 3 + inverse_work,
            )
    received = traded(sent, levels - 1)
    mean, var = run(
        last_kernel,
        [(1, size), (1, size)],
        size,
        flags,
        bits,
        closed,
        received,
        scalars=2,
        extra=inverse_work,
    )
    return mean, var


def solution(mesh):
    return jax.shard_map(
        local,
        mesh=mesh,
        in_specs=(
            P(),
            P(),
            P(),
            P(),
            P("tm", None, None, None),
            P("tm", None, None),
            P("tm", None, None),
            P("tm", None),
            P("tm"),
        ),
        out_specs=(P("tm", None), P("tm", None)),
        check_vma=False,
    )
```

```python
import functools

import jax
import jax.numpy as jnp
from jax import lax
from jax.experimental import pallas as pl
from jax.experimental.pallas import tpu as pltpu
from jax.sharding import PartitionSpec as P

f32 = jnp.float32
bf16 = jnp.bfloat16


def halves(value):
    high = value.astype(bf16)
    return high, (value - high.astype(f32)).astype(bf16)


ROWS = ((1,), (0,))
TURNED = ((1,), (1,))


def mul_halves(left, right, contract=ROWS):
    dims = (contract, ((), ()))
    a, b = left
    c, d = right
    rows = a.shape[0]
    both = lax.dot_general(jnp.concatenate([a, b], axis=0), c, dims, preferred_element_type=f32)
    return both[0:rows] + (both[rows:] + lax.dot_general(a, d, dims, preferred_element_type=f32))


def mul(left, right):
    return mul_halves(halves(left), halves(right))


def mul_nt(left, right):
    return mul_halves(halves(left), halves(right), TURNED)


def stack(*parts):
    return tuple(jnp.concatenate(group, axis=0) for group in zip(*parts))


def masks(size):
    rows = lax.broadcasted_iota(jnp.int32, (size, size), 0)
    cols = lax.broadcasted_iota(jnp.int32, (size, size), 1)
    return rows > cols, rows == cols


def rows8(vector):
    return jnp.broadcast_to(vector, (8, vector.shape[1]))


def invert(m, work):
    size = m.shape[0]
    _, diag = masks(size)
    eye = diag.astype(f32)
    magnitude = jnp.abs(m)
    bound = jnp.max(jnp.sum(magnitude, axis=1, keepdims=True))
    scale = 2.0 / (2.0 + bound)
    work[0:size] = scale * eye
    work[size : 2 * size] = (1.0 - scale) * eye - scale * m

    def step(radius):
        square = radius * radius
        factor = 2.0 / (2.0 - square)
        whole = work[...]
        lower = whole[size : 2 * size]
        ends = jnp.where(diag, lower, 0.0)
        across = jnp.sum(ends, axis=0, keepdims=True)
        down = jnp.sum(ends, axis=1, keepdims=True)
        low = whole.astype(bf16)
        rest = lower - ends
        rest_low = rest.astype(bf16)
        out = jnp.dot(
            jnp.concatenate([low[0:size], rest_low], axis=0), rest_low, preferred_element_type=f32
        )
        work[0:size] = factor * (whole[0:size] * (1.0 + across) + out[0:size])
        work[size : 2 * size] = factor * (
            out[size : 2 * size] + lower * across + rest * down
        ) + (1.0 - factor) * eye
        return square / (2.0 - square)

    lax.while_loop(
        lambda radius: radius > 2e-2, step, jnp.minimum(bound / (2.0 + bound), 1.0 - 1e-6)
    )
    split = halves(m)

    def more(carry):
        square_of, count = carry
        return jnp.logical_and(square_of > 2e-3, count < 60)

    def correct(carry):
        _, count = carry
        x = work[0:size]
        x_halves = halves(x)
        residual = eye - x - mul_halves(x_halves, split)
        low = residual.astype(bf16)
        square = jnp.dot(low, low, preferred_element_type=f32)
        square_of = jnp.max(jnp.sum(jnp.abs(square), axis=0, keepdims=True))
        bad = jnp.logical_and(count == 0, jnp.logical_not(square_of < 0.25))
        better = x + mul_halves(halves(residual + square), x_halves)
        work[0:size] = jnp.where(bad, scale * eye, better)
        return jnp.where(bad, 1.0, square_of), count + 1

    lax.while_loop(more, correct, (jnp.float32(1.0), jnp.int32(0)))
    return work[0:size]


def unpack(tail, linear, square):
    below, diag = masks(square.shape[0])
    turned = square.T
    upto = jnp.logical_or(below, diag)
    info = jnp.where(upto, square, turned)
    cov = jnp.where(upto, turned, square)
    cov = jnp.where(diag, tail[2:3], cov)
    return linear, tail[0:1], cov, tail[1:2], info


def unpack_whole(ref):
    size = ref.shape[1]
    return unpack(ref[0:8], ref[8 : size + 8], ref[size + 8 : 2 * size + 8])


def unpack_halves(got, far, core):
    size = got.shape[1]
    swap = core == 1
    own = got[...]
    other = far[...]
    head = jnp.where(swap, other, own)
    square = jnp.where(swap, own[8:], other[8:])
    return unpack(head[0:8], head[8:], square)


def dual(flag, element):
    linear, offset, cov, vector, info = element
    return (
        jnp.where(flag, linear.T, linear),
        jnp.where(flag, vector, offset),
        jnp.where(flag, info, cov),
        jnp.where(flag, -offset, vector),
        jnp.where(flag, cov, info),
    )


def ordered(flag, one, two):
    return (
        [jnp.where(flag, b, a) for a, b in zip(one, two)],
        [jnp.where(flag, a, b) for a, b in zip(one, two)],
    )


def pack(linear, offset, cov, vector, info):
    size = cov.shape[0]
    below, diag = masks(size)
    square = jnp.where(jnp.logical_or(below, diag), info, cov)
    diagonal = jnp.sum(jnp.where(diag, cov, 0.0), axis=0, keepdims=True)
    tail = jnp.concatenate([offset, vector, diagonal, jnp.zeros((5, size), f32)], axis=0)
    return jnp.concatenate([tail, linear, square], axis=0)


def fold(first, second, work):
    lin1, off1, cov1, vec1, inf1 = first
    lin2, off2, cov2, vec2, inf2 = second
    size = cov1.shape[0]
    cov1_halves = halves(cov1)
    lin1_halves = halves(lin1)
    lin2_halves = halves(lin2)
    inf2_halves = halves(inf2)
    top = mul_halves(stack(cov1_halves, halves(rows8(off1))), inf2_halves)
    pull = halves(rows8(vec2 - top[size : size + 1]))
    weight = halves(invert(top[0:size], work[0]))
    moved = halves(mul_halves(stack(lin2_halves, inf2_halves, pull), weight))
    lin_halves = tuple(part[0:size] for part in moved)
    left = mul_halves(moved, lin1_halves)
    spread = mul_halves(stack(lin_halves, halves(rows8(vec2))), cov1_halves)
    push = off1 + spread[size : size + 1]
    info = inf1 + mul(lin1.T, left[size : 2 * size])
    cov = cov2 + mul_halves(halves(spread[0:size]), lin2_halves, TURNED)
    offset = off2 + mul_halves(halves(rows8(push)), lin_halves, TURNED)[0:1]
    return left[0:size], offset, cov, vec1 + left[2 * size : 2 * size + 1], info


def half_fold(cov1, off1, second, work):
    lin2, off2, cov2, vec2, inf2 = second
    size = cov1.shape[0]
    cov1_halves = halves(cov1)
    lin2_halves = halves(lin2)
    weight = invert(mul_halves(cov1_halves, halves(inf2)), work[0])
    lin_halves = halves(mul_halves(lin2_halves, halves(weight)))
    spread = mul_halves(stack(lin_halves, halves(rows8(vec2))), cov1_halves)
    push = off1 + spread[size : size + 1]
    cov = cov2 + mul_halves(halves(spread[0:size]), lin2_halves, TURNED)
    offset = off2 + mul_halves(halves(rows8(push)), lin_halves, TURNED)[0:1]
    return cov, offset


def build_kernel(flags, trans, op_ref, rows, out, info_ref, work):
    slots, stations, width = op_ref.shape
    size = trans.shape[0]
    step = flags[0]
    value = rows[0:slots]
    noise = rows[slots : 2 * slots]

    def row(index):
        at = 2 * slots + 2 * index
        return jnp.concatenate([rows[at : at + 1], rows[at + 1 : at + 2]], axis=1)

    var_row, mean_row, start_row = row(0), row(1), row(2)
    count = rows[2 * slots + 6 : 2 * slots + 7, 0:1]
    blocks = rows[2 * slots + 7 : 2 * slots + 8]
    noise_cols = noise.T
    weighted = value / noise
    info_ref[...] = jnp.zeros(info_ref.shape, f32)
    infos = [jnp.zeros((width, width), f32) for _ in range(size // width)]
    shifts = [jnp.zeros((1, width), f32) for _ in range(size // width)]
    for m in range(slots):
        op = op_ref[m]
        scaled = (op.astype(f32) / noise_cols[:, m : m + 1]).astype(bf16)
        part = lax.dot_general(scaled, op, (((0,), (0,)), ((), ())), preferred_element_type=f32)
        both = jnp.concatenate(halves(rows8(weighted[m : m + 1])), axis=0)
        both = jnp.dot(both, op, preferred_element_type=f32)
        shift = both[0:1] + both[8:9]
        for a in range(size // width):
            keep = jnp.logical_and(count > m, blocks[:, m : m + 1] == a).astype(f32)
            infos[a] = infos[a] + keep * part
            shifts[a] = shifts[a] + keep * shift
    for a, info in enumerate(infos):
        info = 0.5 * (info + info.T)
        info_ref[a * width : (a + 1) * width, a * width : (a + 1) * width] = info
    h = jnp.concatenate(shifts, axis=1)
    info = info_ref[...]
    first = (step == 0).astype(f32)
    var = first * start_row + (1.0 - first) * var_row
    mean = first * mean_row
    moving = (1.0 - first) * trans[...]
    turned = invert(info * var, work)
    weight = turned.T
    cov = weight * var
    linear = mul(weight, moving)
    small = mul(rows8(h), jnp.concatenate([cov, linear], axis=1))
    offset = small[0:1, 0:size] + mul(rows8(mean), turned)[0:1]
    vector = small[0:1, size : 2 * size]
    info_moved = mul(moving.T, mul(info, linear))
    out[...] = pack(linear, offset, cov, vector, info_moved)


def put_sent(out, sent, core):
    size = out.shape[1]
    sent[...] = out[pl.ds(core * size, size + 8)]


def put_edge(cov, offset, sent):
    size = cov.shape[0]
    part = size // 2
    below, _ = masks(part)
    _, diag = masks(size)
    diagonal = jnp.sum(jnp.where(diag, cov, 0.0), axis=0, keepdims=True)
    sent[0:8] = jnp.concatenate([offset, diagonal, jnp.zeros((6, size), f32)], axis=0)
    shared = jnp.where(below, cov[0:part, 0:part], cov[part:, part:])
    sent[8 : part + 8] = jnp.concatenate([shared, cov[0:part, part:]], axis=1)


def take_edge(ref):
    size = ref.shape[1]
    part = size // 2
    below, _ = masks(part)
    _, diag = masks(size)
    shared = ref[8 : part + 8, 0:part]
    corner = ref[8 : part + 8, part:size]
    turned = shared.T
    cov = jnp.concatenate(
        [
            jnp.concatenate([jnp.where(below, shared, turned), corner], axis=1),
            jnp.concatenate([corner.T, jnp.where(below, turned, shared)], axis=1),
        ],
        axis=0,
    )
    return jnp.where(diag, ref[1:2], cov), ref[0:1]


def pair_kernel(flags, mine, other, state, sent, sides, *work):
    size = mine.shape[1]
    core = flags[1]
    high = core == 1
    own = unpack_whole(mine)
    far = unpack_whole(other)
    whole = pack(*fold(*ordered(high, own, far), work))
    state[...] = whole
    put_sent(state, sent, core)
    _, diag = masks(size)
    eye = diag.astype(f32)
    none = jnp.zeros((8, size), f32)
    neutral = jnp.concatenate([none, eye, jnp.zeros((size, size), f32)], axis=0)
    sides[1] = jnp.where(high, whole, mine[...])
    sides[0] = jnp.where(high, neutral, pack(*dual(jnp.logical_not(high), far)))


def fold_kernel(flags, bits, state, got, far, out, sent, *work):
    core = flags[1]
    high = bits[0] == 1
    received = unpack_halves(got, far, core)
    out[...] = pack(*fold(*ordered(high, unpack_whole(out), received), work))
    put_sent(out, sent, core)


def edge_kernel(flags, bits, state, got, far, sent, *work):
    core = flags[1]
    high = bits[0] == 1
    upper = bits[1] == 1
    first, second = ordered(
        jnp.logical_xor(high, upper), unpack_whole(state), unpack_halves(got, far, core)
    )
    _, offset, cov, _, _ = dual(upper, first)
    cov, offset = half_fold(cov, offset, dual(upper, second), work)
    put_edge(cov, offset, sent)


def side_kernel(flags, bits, sides, got, far, out, *work):
    core = flags[1]
    bit = bits[0]
    received = dual(bit == 0, unpack_halves(got, far, core))
    out[bit] = pack(*fold(received, unpack_whole(out.at[bit]), work))


def two_sides_kernel(flags, bits, sides, got_a, far_a, got_b, far_b, out, received, *work):
    core = flags[1]

    def update(index, carry):
        bit = jnp.where(index == 0, bits[2], bits[0])

        @pl.when(index == 0)
        def _():
            received[...] = pack(*dual(bit == 0, unpack_halves(got_a, far_a, core)))

        @pl.when(index == 1)
        def _():
            received[...] = pack(*dual(bit == 0, unpack_halves(got_b, far_b, core)))

        out[bit] = pack(*fold(unpack_whole(received), unpack_whole(out.at[bit]), work))
        return carry

    lax.fori_loop(0, 2, update, 0)


def close_kernel(flags, bits, sides, got, far, out, one, two, three, *work):
    size = got.shape[1]
    core = flags[1]
    bit = bits[0]
    upper = bits[1] == 1
    _, diag = masks(size)
    one[...] = pack(*dual(bit == 0, unpack_halves(got, far, core)))
    two[...] = sides[bit]

    def turn(index, carry):
        three[...] = pack(*fold(unpack_whole(one), unpack_whole(two), work))

        @pl.when(index == 0)
        def _():
            fresh = unpack_whole(three)
            kept = unpack_whole(sides.at[1 - bit])
            back, front = ordered(bit == 1, fresh, kept)
            eye = diag.astype(f32)
            back_lin, back_off, back_cov, back_vec, back_inf = back
            front_lin, mean, cov, front_vec, front_inf = front
            none = jnp.zeros((1, size), f32)
            zero = jnp.zeros((size, size), f32)
            one[...] = pack(
                jnp.where(upper, front_lin, cov),
                mean,
                cov,
                jnp.where(upper, front_vec, none),
                jnp.where(upper, front_inf, zero),
            )
            two[...] = pack(
                jnp.where(upper, eye, back_lin.T),
                jnp.where(upper, none, -back_vec),
                jnp.where(upper, zero, back_inf),
                back_off,
                back_cov,
            )

        return carry

    lax.fori_loop(0, 2, turn, 0)
    linear, offset, spread, vector, info = unpack_whole(three)
    _, mean, cov, _, _ = unpack_whole(one)
    base = jnp.where(upper, spread, cov - info)
    base = jnp.sum(jnp.where(diag, base, 0.0), axis=0, keepdims=True)
    out[0:8] = jnp.concatenate(
        [
            jnp.where(upper, vector, -offset),
            jnp.where(upper, offset, mean + vector),
            base,
            jnp.zeros((5, size), f32),
        ],
        axis=0,
    )
    out[8 : size + 8] = jnp.where(upper, linear.T, linear)
    out[size + 8 : 2 * size + 8] = jnp.where(upper, info, spread)


def last_kernel(flags, bits, closed, received, mean_out, var_out, work):
    size = received.shape[1]
    sign = (2 * bits[1] - 1).astype(f32)
    matrix, offset = take_edge(received)
    rows = closed[0:8]
    turned = closed[8 : size + 8]
    spread = mul(matrix, turned)
    push = offset + mul(rows8(rows[0:1]), matrix)[0:1]
    weight = invert(mul(matrix, closed[size + 8 : 2 * size + 8]), work)
    moved = mul_nt(rows8(push), weight)
    mean_out[...] = rows[1:2] + mul(moved, turned)[0:1]
    var_out[...] = rows[2:3] + sign * jnp.sum(
        turned * mul(weight, spread), axis=0, keepdims=True
    )


def run(body, out_shapes, size, *args, scalars=0, extra=(), aliases={}):
    vmem = pl.BlockSpec(memory_space=pltpu.VMEM)
    spaces = [
        pl.BlockSpec(memory_space=pltpu.SMEM) if index < scalars else vmem
        for index in range(len(args))
    ]
    single = len(out_shapes) == 1
    shapes = [jax.ShapeDtypeStruct(shape, f32) for shape in out_shapes]
    return pl.pallas_call(
        body,
        out_shape=shapes[0] if single else shapes,
        in_specs=spaces,
        out_specs=vmem if single else [vmem] * len(shapes),
        scratch_shapes=list(extra),
        input_output_aliases=aliases,
        compiler_params=pltpu.CompilerParams(vmem_limit_bytes=16 * 1024 * 1024),
        name=body.__name__,
    )(*args)


def local(
    transition, noise_var, prior_mean, prior_var, obs_op, obs_value, obs_noise, obs_block, obs_count
):
    size = transition.shape[0]
    devices = lax.axis_size("tm")
    levels = (devices - 1).bit_length()
    device = lax.axis_index("tm")
    core = device % 2
    flags = jnp.stack([device, core]).astype(jnp.int32)
    _, slots, stations, width = obs_op.shape
    assert size == 2 * stations
    tall = 2 * slots + 8

    def placed(value, at):
        value = value.astype(f32)
        return jnp.pad(value, ((at, tall - at - value.shape[0]), (0, stations - value.shape[1])))

    rows = (
        placed(obs_value[0], 0)
        + placed(obs_noise[0], slots)
        + placed(noise_var.reshape(2, stations), 2 * slots)
        + placed(prior_mean.reshape(2, stations), 2 * slots + 2)
        + placed(prior_var.reshape(2, stations), 2 * slots + 4)
        + placed(obs_count[:, None], 2 * slots + 6)
        + placed(obs_block, 2 * slots + 7)
    )
    message = (2 * size + 8, size)
    half = (size + 8, size)
    inverse_work = [pltpu.VMEM((2 * size, size), f32)]

    def traded(value, level):
        return lax.ppermute(value, "tm", [(d, d ^ (1 << level)) for d in range(devices)])

    element = run(
        build_kernel,
        [message],
        size,
        flags,
        transition,
        obs_op[0],
        rows,
        scalars=1,
        extra=[pltpu.VMEM((size, size), f32)] + inverse_work,
    )
    other = traded(element, 0)
    state, sent, sides = run(
        pair_kernel,
        [message, half, (2,) + message],
        size,
        flags,
        element,
        other,
        scalars=1,
        extra=inverse_work,
    )
    for level in range(1, levels - 1):
        bits = jnp.stack([(device >> (level + k)) % 2 for k in (0, 1, -1)]).astype(jnp.int32)
        got = traded(sent, level)
        got, sides = lax.optimization_barrier((got, sides))
        far = traded(got, 0)
        now = (flags, bits, state, got, far)
        if level < levels - 2:
            state, sent = run(
                fold_kernel,
                [message, half],
                size,
                *now,
                scalars=2,
                extra=inverse_work,
                aliases={2: 0},
            )
        else:
            sent = run(edge_kernel, [(size // 2 + 8, size)], size, *now, scalars=2, extra=inverse_work)
        _, sides = lax.optimization_barrier((sent, sides))
        now = (flags, bits, sides, got, far)
        if level % 2 == 1 and level < levels - 3:
            waiting = (got, far)
        elif level % 2 == 0 and level < levels - 2:
            sides = run(
                two_sides_kernel,
                [(2,) + message],
                size,
                flags,
                bits,
                sides,
                *waiting,
                got,
                far,
                scalars=2,
                extra=[pltpu.VMEM(message, f32)] + inverse_work,
                aliases={2: 0},
            )
        elif level < levels - 2:
            sides = run(
                side_kernel,
                [(2,) + message],
                size,
                *now,
                scalars=2,
                extra=inverse_work,
                aliases={2: 0},
            )
        else:
            closed = run(
                close_kernel,
                [message],
                size,
                *now,
                scalars=2,
                extra=[pltpu.VMEM(message, f32)] * 3 + inverse_work,
            )
    received = traded(sent, levels - 1)
    mean, var = run(
        last_kernel,
        [(1, size), (1, size)],
        size,
        flags,
        bits,
        closed,
        received,
        scalars=2,
        extra=inverse_work,
    )
    return mean, var


def solution(mesh):
    return jax.shard_map(
        local,
        mesh=mesh,
        in_specs=(
            P(),
            P(),
            P(),
            P(),
            P("tm", None, None, None),
            P("tm", None, None),
            P("tm", None, None),
            P("tm", None),
            P("tm"),
        ),
        out_specs=(P("tm", None), P("tm", None)),
        check_vma=False,
    )
```

```python
import functools

import jax
import jax.numpy as jnp
from jax import lax
from jax.experimental import pallas as pl
from jax.experimental.pallas import tpu as pltpu
from jax.sharding import PartitionSpec as P

f32 = jnp.float32
bf16 = jnp.bfloat16


def halves(value):
    high = value.astype(bf16)
    return high, (value - high.astype(f32)).astype(bf16)


ROWS = ((1,), (0,))
TURNED = ((1,), (1,))


def mul_halves(left, right, contract=ROWS):
    dims = (contract, ((), ()))
    a, b = left
    c, d = right
    rows = a.shape[0]
    both = lax.dot_general(jnp.concatenate([a, b], axis=0), c, dims, preferred_element_type=f32)
    return both[0:rows] + (both[rows:] + lax.dot_general(a, d, dims, preferred_element_type=f32))


def mul(left, right):
    return mul_halves(halves(left), halves(right))


def mul_nt(left, right):
    return mul_halves(halves(left), halves(right), TURNED)


def stack(*parts):
    return tuple(jnp.concatenate(group, axis=0) for group in zip(*parts))


def masks(size):
    rows = lax.broadcasted_iota(jnp.int32, (size, size), 0)
    cols = lax.broadcasted_iota(jnp.int32, (size, size), 1)
    return rows > cols, rows == cols


def rows8(vector):
    return jnp.broadcast_to(vector, (8, vector.shape[1]))


def invert(m, work):
    size = m.shape[0]
    _, diag = masks(size)
    eye = diag.astype(f32)
    magnitude = jnp.abs(m)
    bound = jnp.max(jnp.sum(magnitude, axis=1, keepdims=True))
    scale = 2.0 / (2.0 + bound)
    work[0:size] = scale * eye
    work[size : 2 * size] = (1.0 - scale) * eye - scale * m

    def step(radius):
        square = radius * radius
        factor = 2.0 / (2.0 - square)
        whole = work[...]
        lower = whole[size : 2 * size]
        ends = jnp.where(diag, lower, 0.0)
        across = jnp.sum(ends, axis=0, keepdims=True)
        down = jnp.sum(ends, axis=1, keepdims=True)
        low = whole.astype(bf16)
        rest = lower - ends
        rest_low = rest.astype(bf16)
        out = jnp.dot(
            jnp.concatenate([low[0:size], rest_low], axis=0), rest_low, preferred_element_type=f32
        )
        work[0:size] = factor * (whole[0:size] * (1.0 + across) + out[0:size])
        work[size : 2 * size] = factor * (
            out[size : 2 * size] + lower * across + rest * down
        ) + (1.0 - factor) * eye
        return square / (2.0 - square)

    lax.while_loop(
        lambda radius: radius > 1e-2, step, jnp.minimum(bound / (2.0 + bound), 1.0 - 1e-6)
    )
    split = halves(m)

    def more(carry):
        square_of, count = carry
        return jnp.logical_and(square_of > 5e-3, count < 60)

    def correct(carry):
        _, count = carry
        x = work[0:size]
        x_halves = halves(x)
        residual = eye - x - mul_halves(x_halves, split)
        low = residual.astype(bf16)
        square = jnp.dot(low, low, preferred_element_type=f32)
        square_of = jnp.max(jnp.sum(jnp.abs(square), axis=0, keepdims=True))
        bad = jnp.logical_and(count == 0, jnp.logical_not(square_of < 0.25))
        better = x + mul_halves(halves(residual + square), x_halves)
        work[0:size] = jnp.where(bad, scale * eye, better)
        return jnp.where(bad, 1.0, square_of), count + 1

    lax.while_loop(more, correct, (jnp.float32(1.0), jnp.int32(0)))
    return work[0:size]


def unpack(tail, linear, square):
    below, diag = masks(square.shape[0])
    turned = square.T
    upto = jnp.logical_or(below, diag)
    info = jnp.where(upto, square, turned)
    cov = jnp.where(upto, turned, square)
    cov = jnp.where(diag, tail[2:3], cov)
    return linear, tail[0:1], cov, tail[1:2], info


def unpack_whole(ref):
    size = ref.shape[1]
    return unpack(ref[0:8], ref[8 : size + 8], ref[size + 8 : 2 * size + 8])


def unpack_halves(got, far, core):
    size = got.shape[1]
    swap = core == 1
    own = got[...]
    other = far[...]
    head = jnp.where(swap, other, own)
    square = jnp.where(swap, own[8:], other[8:])
    return unpack(head[0:8], head[8:], square)


def dual(flag, element):
    linear, offset, cov, vector, info = element
    return (
        jnp.where(flag, linear.T, linear),
        jnp.where(flag, vector, offset),
        jnp.where(flag, info, cov),
        jnp.where(flag, -offset, vector),
        jnp.where(flag, cov, info),
    )


def ordered(flag, one, two):
    return (
        [jnp.where(flag, b, a) for a, b in zip(one, two)],
        [jnp.where(flag, a, b) for a, b in zip(one, two)],
    )


def pack(linear, offset, cov, vector, info):
    size = cov.shape[0]
    below, diag = masks(size)
    square = jnp.where(jnp.logical_or(below, diag), info, cov)
    diagonal = jnp.sum(jnp.where(diag, cov, 0.0), axis=0, keepdims=True)
    tail = jnp.concatenate([offset, vector, diagonal, jnp.zeros((5, size), f32)], axis=0)
    return jnp.concatenate([tail, linear, square], axis=0)


def fold(first, second, work):
    lin1, off1, cov1, vec1, inf1 = first
    lin2, off2, cov2, vec2, inf2 = second
    size = cov1.shape[0]
    cov1_halves = halves(cov1)
    lin1_halves = halves(lin1)
    lin2_halves = halves(lin2)
    inf2_halves = halves(inf2)
    top = mul_halves(stack(cov1_halves, halves(rows8(off1))), inf2_halves)
    pull = halves(rows8(vec2 - top[size : size + 1]))
    weight = halves(invert(top[0:size], work[0]))
    moved = halves(mul_halves(stack(lin2_halves, inf2_halves, pull), weight))
    lin_halves = tuple(part[0:size] for part in moved)
    left = mul_halves(moved, lin1_halves)
    spread = mul_halves(stack(lin_halves, halves(rows8(vec2))), cov1_halves)
    push = off1 + spread[size : size + 1]
    info = inf1 + mul(lin1.T, left[size : 2 * size])
    cov = cov2 + mul_halves(halves(spread[0:size]), lin2_halves, TURNED)
    offset = off2 + mul_halves(halves(rows8(push)), lin_halves, TURNED)[0:1]
    return left[0:size], offset, cov, vec1 + left[2 * size : 2 * size + 1], info


def half_fold(cov1, off1, second, work):
    lin2, off2, cov2, vec2, inf2 = second
    size = cov1.shape[0]
    cov1_halves = halves(cov1)
    lin2_halves = halves(lin2)
    weight = invert(mul_halves(cov1_halves, halves(inf2)), work[0])
    lin_halves = halves(mul_halves(lin2_halves, halves(weight)))
    spread = mul_halves(stack(lin_halves, halves(rows8(vec2))), cov1_halves)
    push = off1 + spread[size : size + 1]
    cov = cov2 + mul_halves(halves(spread[0:size]), lin2_halves, TURNED)
    offset = off2 + mul_halves(halves(rows8(push)), lin_halves, TURNED)[0:1]
    return cov, offset


def build_kernel(flags, trans, op_ref, rows, out, info_ref, work):
    slots, stations, width = op_ref.shape
    size = trans.shape[0]
    step = flags[0]
    value = rows[0:slots]
    noise = rows[slots : 2 * slots]

    def row(index):
        at = 2 * slots + 2 * index
        return jnp.concatenate([rows[at : at + 1], rows[at + 1 : at + 2]], axis=1)

    var_row, mean_row, start_row = row(0), row(1), row(2)
    count = rows[2 * slots + 6 : 2 * slots + 7, 0:1]
    blocks = rows[2 * slots + 7 : 2 * slots + 8]
    noise_cols = noise.T
    weighted = value / noise
    info_ref[...] = jnp.zeros(info_ref.shape, f32)
    infos = [jnp.zeros((width, width), f32) for _ in range(size // width)]
    shifts = [jnp.zeros((1, width), f32) for _ in range(size // width)]
    for m in range(slots):
        op = op_ref[m]
        scaled = (op.astype(f32) / noise_cols[:, m : m + 1]).astype(bf16)
        part = lax.dot_general(scaled, op, (((0,), (0,)), ((), ())), preferred_element_type=f32)
        both = jnp.concatenate(halves(rows8(weighted[m : m + 1])), axis=0)
        both = jnp.dot(both, op, preferred_element_type=f32)
        shift = both[0:1] + both[8:9]
        for a in range(size // width):
            keep = jnp.logical_and(count > m, blocks[:, m : m + 1] == a).astype(f32)
            infos[a] = infos[a] + keep * part
            shifts[a] = shifts[a] + keep * shift
    for a, info in enumerate(infos):
        info = 0.5 * (info + info.T)
        info_ref[a * width : (a + 1) * width, a * width : (a + 1) * width] = info
    h = jnp.concatenate(shifts, axis=1)
    info = info_ref[...]
    first = (step == 0).astype(f32)
    var = first * start_row + (1.0 - first) * var_row
    mean = first * mean_row
    moving = (1.0 - first) * trans[...]
    turned = invert(info * var, work)
    weight = turned.T
    cov = weight * var
    linear = mul(weight, moving)
    small = mul(rows8(h), jnp.concatenate([cov, linear], axis=1))
    offset = small[0:1, 0:size] + mul(rows8(mean), turned)[0:1]
    vector = small[0:1, size : 2 * size]
    info_moved = mul(moving.T, mul(info, linear))
    out[...] = pack(linear, offset, cov, vector, info_moved)


def put_sent(out, sent, core):
    size = out.shape[1]
    sent[...] = out[pl.ds(core * size, size + 8)]


def put_edge(cov, offset, sent):
    size = cov.shape[0]
    part = size // 2
    below, _ = masks(part)
    _, diag = masks(size)
    diagonal = jnp.sum(jnp.where(diag, cov, 0.0), axis=0, keepdims=True)
    sent[0:8] = jnp.concatenate([offset, diagonal, jnp.zeros((6, size), f32)], axis=0)
    shared = jnp.where(below, cov[0:part, 0:part], cov[part:, part:])
    sent[8 : part + 8] = jnp.concatenate([shared, cov[0:part, part:]], axis=1)


def take_edge(ref):
    size = ref.shape[1]
    part = size // 2
    below, _ = masks(part)
    _, diag = masks(size)
    shared = ref[8 : part + 8, 0:part]
    corner = ref[8 : part + 8, part:size]
    turned = shared.T
    cov = jnp.concatenate(
        [
            jnp.concatenate([jnp.where(below, shared, turned), corner], axis=1),
            jnp.concatenate([corner.T, jnp.where(below, turned, shared)], axis=1),
        ],
        axis=0,
    )
    return jnp.where(diag, ref[1:2], cov), ref[0:1]


def pair_kernel(flags, mine, other, state, sent, sides, *work):
    size = mine.shape[1]
    core = flags[1]
    high = core == 1
    own = unpack_whole(mine)
    far = unpack_whole(other)
    whole = pack(*fold(*ordered(high, own, far), work))
    state[...] = whole
    put_sent(state, sent, core)
    _, diag = masks(size)
    eye = diag.astype(f32)
    none = jnp.zeros((8, size), f32)
    neutral = jnp.concatenate([none, eye, jnp.zeros((size, size), f32)], axis=0)
    sides[1] = jnp.where(high, whole, mine[...])
    sides[0] = jnp.where(high, neutral, pack(*dual(jnp.logical_not(high), far)))


def fold_kernel(flags, bits, state, got, far, out, sent, *work):
    core = flags[1]
    high = bits[0] == 1
    received = unpack_halves(got, far, core)
    out[...] = pack(*fold(*ordered(high, unpack_whole(out), received), work))
    put_sent(out, sent, core)


def edge_kernel(flags, bits, state, got, far, sent, *work):
    core = flags[1]
    high = bits[0] == 1
    upper = bits[1] == 1
    first, second = ordered(
        jnp.logical_xor(high, upper), unpack_whole(state), unpack_halves(got, far, core)
    )
    _, offset, cov, _, _ = dual(upper, first)
    cov, offset = half_fold(cov, offset, dual(upper, second), work)
    put_edge(cov, offset, sent)


def side_kernel(flags, bits, sides, got, far, out, *work):
    core = flags[1]
    bit = bits[0]
    received = dual(bit == 0, unpack_halves(got, far, core))
    out[bit] = pack(*fold(received, unpack_whole(out.at[bit]), work))


def two_sides_kernel(flags, bits, sides, got_a, far_a, got_b, far_b, out, received, *work):
    core = flags[1]

    def update(index, carry):
        bit = jnp.where(index == 0, bits[2], bits[0])

        @pl.when(index == 0)
        def _():
            received[...] = pack(*dual(bit == 0, unpack_halves(got_a, far_a, core)))

        @pl.when(index == 1)
        def _():
            received[...] = pack(*dual(bit == 0, unpack_halves(got_b, far_b, core)))

        out[bit] = pack(*fold(unpack_whole(received), unpack_whole(out.at[bit]), work))
        return carry

    lax.fori_loop(0, 2, update, 0)


def close_kernel(flags, bits, sides, got, far, out, one, two, three, *work):
    size = got.shape[1]
    core = flags[1]
    bit = bits[0]
    upper = bits[1] == 1
    _, diag = masks(size)
    one[...] = pack(*dual(bit == 0, unpack_halves(got, far, core)))
    two[...] = sides[bit]

    def turn(index, carry):
        three[...] = pack(*fold(unpack_whole(one), unpack_whole(two), work))

        @pl.when(index == 0)
        def _():
            fresh = unpack_whole(three)
            kept = unpack_whole(sides.at[1 - bit])
            back, front = ordered(bit == 1, fresh, kept)
            eye = diag.astype(f32)
            back_lin, back_off, back_cov, back_vec, back_inf = back
            front_lin, mean, cov, front_vec, front_inf = front
            none = jnp.zeros((1, size), f32)
            zero = jnp.zeros((size, size), f32)
            one[...] = pack(
                jnp.where(upper, front_lin, cov),
                mean,
                cov,
                jnp.where(upper, front_vec, none),
                jnp.where(upper, front_inf, zero),
            )
            two[...] = pack(
                jnp.where(upper, eye, back_lin.T),
                jnp.where(upper, none, -back_vec),
                jnp.where(upper, zero, back_inf),
                back_off,
                back_cov,
            )

        return carry

    lax.fori_loop(0, 2, turn, 0)
    linear, offset, spread, vector, info = unpack_whole(three)
    _, mean, cov, _, _ = unpack_whole(one)
    base = jnp.where(upper, spread, cov - info)
    base = jnp.sum(jnp.where(diag, base, 0.0), axis=0, keepdims=True)
    out[0:8] = jnp.concatenate(
        [
            jnp.where(upper, vector, -offset),
            jnp.where(upper, offset, mean + vector),
            base,
            jnp.zeros((5, size), f32),
        ],
        axis=0,
    )
    out[8 : size + 8] = jnp.where(upper, linear.T, linear)
    out[size + 8 : 2 * size + 8] = jnp.where(upper, info, spread)


def last_kernel(flags, bits, closed, received, mean_out, var_out, work):
    size = received.shape[1]
    sign = (2 * bits[1] - 1).astype(f32)
    matrix, offset = take_edge(received)
    rows = closed[0:8]
    turned = closed[8 : size + 8]
    spread = mul(matrix, turned)
    push = offset + mul(rows8(rows[0:1]), matrix)[0:1]
    weight = invert(mul(matrix, closed[size + 8 : 2 * size + 8]), work)
    moved = mul_nt(rows8(push), weight)
    mean_out[...] = rows[1:2] + mul(moved, turned)[0:1]
    var_out[...] = rows[2:3] + sign * jnp.sum(
        turned * mul(weight, spread), axis=0, keepdims=True
    )


def run(body, out_shapes, size, *args, scalars=0, extra=(), aliases={}):
    vmem = pl.BlockSpec(memory_space=pltpu.VMEM)
    spaces = [
        pl.BlockSpec(memory_space=pltpu.SMEM) if index < scalars else vmem
        for index in range(len(args))
    ]
    single = len(out_shapes) == 1
    shapes = [jax.ShapeDtypeStruct(shape, f32) for shape in out_shapes]
    return pl.pallas_call(
        body,
        out_shape=shapes[0] if single else shapes,
        in_specs=spaces,
        out_specs=vmem if single else [vmem] * len(shapes),
        scratch_shapes=list(extra),
        input_output_aliases=aliases,
        compiler_params=pltpu.CompilerParams(vmem_limit_bytes=16 * 1024 * 1024),
        name=body.__name__,
    )(*args)


def local(
    transition, noise_var, prior_mean, prior_var, obs_op, obs_value, obs_noise, obs_block, obs_count
):
    size = transition.shape[0]
    devices = lax.axis_size("tm")
    levels = (devices - 1).bit_length()
    device = lax.axis_index("tm")
    core = device % 2
    flags = jnp.stack([device, core]).astype(jnp.int32)
    _, slots, stations, width = obs_op.shape
    assert size == 2 * stations
    tall = 2 * slots + 8

    def placed(value, at):
        value = value.astype(f32)
        return jnp.pad(value, ((at, tall - at - value.shape[0]), (0, stations - value.shape[1])))

    rows = (
        placed(obs_value[0], 0)
        + placed(obs_noise[0], slots)
        + placed(noise_var.reshape(2, stations), 2 * slots)
        + placed(prior_mean.reshape(2, stations), 2 * slots + 2)
        + placed(prior_var.reshape(2, stations), 2 * slots + 4)
        + placed(obs_count[:, None], 2 * slots + 6)
        + placed(obs_block, 2 * slots + 7)
    )
    message = (2 * size + 8, size)
    half = (size + 8, size)
    inverse_work = [pltpu.VMEM((2 * size, size), f32)]

    def traded(value, level):
        return lax.ppermute(value, "tm", [(d, d ^ (1 << level)) for d in range(devices)])

    element = run(
        build_kernel,
        [message],
        size,
        flags,
        transition,
        obs_op[0],
        rows,
        scalars=1,
        extra=[pltpu.VMEM((size, size), f32)] + inverse_work,
    )
    other = traded(element, 0)
    state, sent, sides = run(
        pair_kernel,
        [message, half, (2,) + message],
        size,
        flags,
        element,
        other,
        scalars=1,
        extra=inverse_work,
    )
    for level in range(1, levels - 1):
        bits = jnp.stack([(device >> (level + k)) % 2 for k in (0, 1, -1)]).astype(jnp.int32)
        got = traded(sent, level)
        got, sides = lax.optimization_barrier((got, sides))
        far = traded(got, 0)
        now = (flags, bits, state, got, far)
        if level < levels - 2:
            state, sent = run(
                fold_kernel,
                [message, half],
                size,
                *now,
                scalars=2,
                extra=inverse_work,
                aliases={2: 0},
            )
        else:
            sent = run(edge_kernel, [(size // 2 + 8, size)], size, *now, scalars=2, extra=inverse_work)
        _, sides = lax.optimization_barrier((sent, sides))
        now = (flags, bits, sides, got, far)
        if level % 2 == 1 and level < levels - 3:
            waiting = (got, far)
        elif level % 2 == 0 and level < levels - 2:
            sides = run(
                two_sides_kernel,
                [(2,) + message],
                size,
                flags,
                bits,
                sides,
                *waiting,
                got,
                far,
                scalars=2,
                extra=[pltpu.VMEM(message, f32)] + inverse_work,
                aliases={2: 0},
            )
        elif level < levels - 2:
            sides = run(
                side_kernel,
                [(2,) + message],
                size,
                *now,
                scalars=2,
                extra=inverse_work,
                aliases={2: 0},
            )
        else:
            closed = run(
                close_kernel,
                [message],
                size,
                *now,
                scalars=2,
                extra=[pltpu.VMEM(message, f32)] * 3 + inverse_work,
            )
    received = traded(sent, levels - 1)
    mean, var = run(
        last_kernel,
        [(1, size), (1, size)],
        size,
        flags,
        bits,
        closed,
        received,
        scalars=2,
        extra=inverse_work,
    )
    return mean, var


def solution(mesh):
    return jax.shard_map(
        local,
        mesh=mesh,
        in_specs=(
            P(),
            P(),
            P(),
            P(),
            P("tm", None, None, None),
            P("tm", None, None),
            P("tm", None, None),
            P("tm", None),
            P("tm"),
        ),
        out_specs=(P("tm", None), P("tm", None)),
        check_vma=False,
    )
```
